512 devices in a mesh: ctx: 128 (over y, z, x_lo), tp: 4 (over x_hi, core).
Axes of the slice: x: 4 (x_hi: 2, x_lo: 2; x = x_hi * 2 + x_lo), y: 8, z: 8, core: 2. Of those that a mesh axis runs over, the one named last changes fastest.
Arguments:
- features: bfloat16 [3, 2048, 16384], P(None, 'tp', 'ctx'), may hold values from -6 to 6
- short_taps: float32 [3, 3, 2048], P(None, None, 'tp'), may hold values from -3 to 3
- filters: bfloat16 [128, 16384], P('tp'), may hold values from -2 to 2
- skip_gain: float32 [2048], P('tp'), may hold values from -4 to 4
- out_weight: bfloat16 [2048, 2048], P('tp'), may hold values from -0.125 to 0.125
Outputs:
- block_out: bfloat16 [2048, 16384], P('tp', 'ctx')
The draws below stay inside these ranges and needn't reach their ends.
All inputs are finite; a program needn't handle non-finite values.
Results may differ from the reference program's by a relative error of at most 0.009.
Values may be sent and summed in bfloat16 or wider, within the bound.
No kernel may reach another device: no remote copies, remote signals or barrier semaphores. Data moves between devices by JAX's collectives and lax.ppermute only.
A program may use at most 64 MiB of HBM per device.

```python
import math
import jax
import jax.numpy as jnp
from jax import lax

CH = 2048
OUT = 2048
GROUP = 16
TAPS = 3
GROUPS = 128
TOKENS = 16384
N_TP = 4


def draw_filters(key, part):
    rate_key, value_key = jax.random.split(jax.random.fold_in(key, 17))
    position = jnp.arange(TOKENS, dtype=jnp.float32)
    log_span = jax.random.uniform(rate_key, (GROUPS, 1), minval=math.log(30.0), maxval=math.log(TOKENS * 4.0))
    values = jax.random.normal(value_key, (GROUPS, TOKENS))
    span_len = jnp.exp(log_span)
    envelope = jnp.exp(-position[None, :] / span_len)
    energy = (1.0 - jnp.exp(-2.0 / span_len)) / (1.0 - jnp.exp(-2.0 * TOKENS / span_len))
    return (values * envelope * jnp.sqrt(energy)).astype(jnp.float32).astype(jnp.bfloat16)


def steps_of(own_key, dims, pieces, least, largest):
    loudness = 1.0
    for dim, shards_of in pieces:
        steps = jax.random.uniform(jax.random.fold_in(jax.random.fold_in(own_key, 6), dim), (shards_of,), jnp.float32, least / len(pieces), largest / len(pieces))
        loudness = loudness * jnp.repeat(jnp.exp(steps), dims[dim] // shards_of).reshape((-1,) + (1,) * (len(dims) - 1 - dim))
    return loudness


def scatter_about(stream_key, dims, deviation, bound, shards=(), kind=jnp.bfloat16):
    array = deviation * jax.random.normal(stream_key, dims, jnp.float32)
    if shards:
        array = array * steps_of(stream_key, dims, shards, -0.22, 0.18)
    return jnp.clip(array, -bound, bound).astype(kind)


def setup_inputs(seed: int = 0) -> dict:
    streams_of = jax.random.split(jax.random.key(seed), 6)
    return {
        "features": scatter_about(streams_of[0], (3, CH, TOKENS), 1.0, 6.0, ((1, 4), (2, 128))),
        "short_taps": scatter_about(streams_of[1], (TAPS, 3, CH), 0.6, 3.0, ((2, 4),), jnp.float32),
        "filters": draw_filters(jax.random.fold_in(streams_of[5], 71), 0),
        "skip_gain": scatter_about(streams_of[3], (CH,), 1.0, 4.0, ((0, 4),), jnp.float32),
        "out_weight": scatter_about(streams_of[4], (CH, OUT), CH ** -0.5, 0.125, ((0, 4),)),
    }


def short_conv(features, short_taps):
    taps_count = short_taps.shape[0]
    values = features.astype(jnp.float32)
    padded = jnp.pad(values, ((0, 0), (0, 0), (taps_count - 1, 0)))
    length = values.shape[2]
    result = jnp.zeros(values.shape, jnp.float32)
    for offset in range(taps_count):
        begin_at = taps_count - 1 - offset
        result = result + short_taps[offset][:, :, None] * padded[:, :, begin_at:begin_at + length]
    return result


def group_conv(operands):
    signal, kernel = operands
    fft_size = 2 * TOKENS
    spectrum = jnp.fft.rfft(signal.astype(jnp.float32), n=fft_size) * jnp.fft.rfft(kernel.astype(jnp.float32), n=fft_size)[None, :]
    return jnp.fft.irfft(spectrum, n=fft_size)[:, :TOKENS]


def reference(features, short_taps, filters, skip_gain, out_weight):
    conv_all = short_conv(features, short_taps)
    query_conv = conv_all[0]
    product = (conv_all[1] * conv_all[2]).astype(jnp.bfloat16)
    grouped = product.reshape(GROUPS, GROUP, TOKENS)
    longconv = lax.map(group_conv, (grouped, filters)).reshape(CH, TOKENS)
    long_mix = (longconv + skip_gain[:, None] * product.astype(jnp.float32)).astype(jnp.bfloat16)
    gated = (query_conv * long_mix.astype(jnp.float32)).astype(jnp.bfloat16)
    block_width = CH // N_TP
    summed = jnp.zeros((OUT, TOKENS), jnp.float32)
    for member in range(N_TP):
        weight_rows = out_weight[member * block_width:(member + 1) * block_width]
        gated_rows = gated[member * block_width:(member + 1) * block_width]
        partial_sum = jnp.dot(weight_rows.T, gated_rows, preferred_element_type=jnp.float32)
        rounded = lax.optimization_barrier(partial_sum.astype(jnp.bfloat16))
        summed = summed + rounded.astype(jnp.float32)
    return summed.astype(jnp.bfloat16)
```

```python
import jax
import jax.numpy as jnp
from jax import lax
from jax.experimental import pallas as pl
from jax.experimental.pallas import tpu as pltpu
from jax.sharding import PartitionSpec as P

GROUP = 16
LANES = 128
CHUNK = 1024

f32 = jnp.float32
bf16 = jnp.bfloat16


def pattern(values):
    row = lax.broadcasted_iota(jnp.int32, (8, LANES), 0) % 4
    tile = jnp.full((8, LANES), values[3], f32)
    for index in (2, 1, 0):
        tile = jnp.where(row == index, values[index], tile)
    return tile


def by_rows(tile, array):
    rows = array.shape[0]
    return (array.reshape(rows // 8, 8, LANES) * tile[None]).reshape(rows, LANES)


def short_conv(value, tiles):
    lane = lax.broadcasted_iota(jnp.int32, value.shape, 1)
    row = lax.broadcasted_iota(jnp.int32, value.shape, 0)
    total = by_rows(tiles[0], value)
    for offset in (1, 2):
        turned = pltpu.roll(value, offset, 1)
        before = jnp.where(row < 4, 0.0, pltpu.roll(turned, 4, 0))
        total = total + by_rows(tiles[offset], jnp.where(lane < offset, before, turned))
    return total


def conv_kernel(rank_ref, q_ref, k_ref, v_ref, filter_ref, taps_ref, skip_ref, out_ref, line_ref, table_ref, pair_ref, sum_ref):
    rank = rank_ref[0]
    first = rank * 4
    rows = q_ref.shape[0]
    seq_len = filter_ref.shape[1]

    def tiles_of(feature):
        return [pattern([taps_ref[offset, feature, first + c] for c in range(4)]) for offset in range(3)]

    k_conv = short_conv(k_ref[...].astype(f32), tiles_of(1))
    v_conv = short_conv(v_ref[...].astype(f32), tiles_of(2))
    kv = (k_conv * v_conv).astype(bf16).astype(f32)
    row = lax.broadcasted_iota(jnp.int32, kv.shape, 0)
    pair_ref[:, :LANES] = kv.astype(bf16)
    pair_ref[:, LANES:] = jnp.where(row < 4, 0.0, pltpu.roll(kv, 4, 0)).astype(bf16)

    own = (rank * 4 // GROUP) % 8
    line_ref[:, :LANES] = jnp.zeros((8, LANES), f32)
    for at in range(0, seq_len, CHUNK):
        piece = filter_ref[:, at : at + CHUNK].astype(f32)
        sub = lax.broadcasted_iota(jnp.int32, piece.shape, 0)
        chosen = jnp.sum(jnp.where(sub == own, piece, 0.0), axis=0, keepdims=True)
        line_ref[:, LANES + at : LANES + at + CHUNK] = jnp.broadcast_to(chosen, piece.shape)

    sum_ref[...] = jnp.zeros_like(sum_ref)
    for at in range(0, seq_len, CHUNK):
        piece = pltpu.roll(line_ref[:, at : at + CHUNK + LANES], 0, 1, stride=1, stride_axis=0)
        for tile in range(LANES // 16):
            upper = pltpu.roll(piece, 16 * tile, 1)[:, LANES:]
            lower = pltpu.roll(piece, 16 * tile + 8, 1)[:, LANES:]
            both = jnp.concatenate([upper, lower], axis=0).astype(bf16)
            for block in range(CHUNK // LANES):
                to_row = (block % 2) * LANES + 16 * tile
                to_col = (at // LANES + block) // 2 * LANES
                table_ref[to_row : to_row + 16, to_col : to_col + LANES] = both[:, block * LANES : (block + 1) * LANES]
        for part in range(CHUNK // 512):
            begin = (at // 512 + part) * 16
            moved = jnp.dot(
                pair_ref[: rows - begin, :],
                table_ref[:, begin * 16 : begin * 16 + 256],
                preferred_element_type=f32,
            )
            sum_ref[begin:, :] += moved[:, :LANES]
            sum_ref[begin + 8 :, :] += moved[: rows - begin - 8, LANES:]

    direct = pattern([skip_ref[first + c] for c in range(4)])
    kv = pair_ref[:, :LANES].astype(f32)
    long_mix = (sum_ref[...] + by_rows(direct, kv)).astype(bf16).astype(f32)
    q_conv = short_conv(q_ref[...].astype(f32), tiles_of(0))
    out_ref[...] = (q_conv * long_mix).astype(bf16)


def long_conv(rank, q, k, v, filters, short_taps, skip_gain):
    rows = q.shape[0]
    seq_len = filters.shape[1]
    whole = pl.BlockSpec((rows, LANES), lambda i, r: (0, 0))
    in_smem = pl.BlockSpec(memory_space=pltpu.SMEM)
    return pl.pallas_call(
        conv_kernel,
        out_shape=jax.ShapeDtypeStruct((rows, LANES), bf16),
        grid_spec=pltpu.PrefetchScalarGridSpec(
            num_scalar_prefetch=1,
            grid=(1,),
            in_specs=[
                whole,
                whole,
                whole,
                pl.BlockSpec((8, seq_len), lambda i, r: (r[0] * 4 // GROUP // 8, 0)),
                in_smem,
                in_smem,
            ],
            out_specs=whole,
            scratch_shapes=[
                pltpu.VMEM((8, LANES + seq_len), f32),
                pltpu.VMEM((2 * LANES, seq_len // 2), bf16),
                pltpu.VMEM((rows, 2 * LANES), bf16),
                pltpu.VMEM((rows, LANES), f32),
            ],
        ),
        cost_estimate=pl.CostEstimate(flops=1 << 31, bytes_accessed=1 << 20, transcendentals=0),
        name="long_conv",
    )(rank, q, k, v, filters, short_taps, skip_gain)


def project_kernel(gated_ref, weight_ref, out_ref):
    turned = jnp.transpose(gated_ref[...].astype(f32)).astype(bf16)
    width = out_ref.shape[2]
    for member in range(out_ref.shape[0]):
        out_ref[member] = jnp.dot(
            turned, weight_ref[:, member * width : (member + 1) * width], preferred_element_type=f32
        ).astype(bf16)


def project(gated, weight, members):
    return pl.pallas_call(
        project_kernel,
        out_shape=jax.ShapeDtypeStruct((members, gated.shape[1], weight.shape[1] // members), bf16),
        cost_estimate=pl.CostEstimate(flops=1 << 28, bytes_accessed=1 << 21, transcendentals=0),
        name="project",
    )(gated, weight)


def combine_kernel(parts_ref, out_ref):
    total = parts_ref[0].astype(f32)
    for member in range(1, parts_ref.shape[0]):
        total = total + parts_ref[member].astype(f32)
    out_ref[...] = jnp.transpose(total).astype(bf16)


def combine(parts):
    return pl.pallas_call(
        combine_kernel,
        out_shape=jax.ShapeDtypeStruct((parts.shape[2], parts.shape[1]), bf16),
        cost_estimate=pl.CostEstimate(flops=1 << 20, bytes_accessed=1 << 19, transcendentals=0),
        name="combine",
    )(parts)


def local(features, short_taps, filters, skip_gain, out_weight):
    rows_in, chan_tp, tok_local = features.shape
    ctx_count = lax.axis_size("ctx")
    tp_count = lax.axis_size("tp")
    chan_dev = chan_tp // ctx_count
    rank = jnp.full((1,), lax.axis_index("ctx"), jnp.int32)
    sent = features.reshape(rows_in, ctx_count, chan_dev, tok_local).transpose(1, 0, 2, 3)
    sent = sent.reshape(ctx_count, rows_in * chan_dev, tok_local)
    got = lax.all_to_all(sent, "ctx", 0, 0, tiled=True)
    got = got.reshape(ctx_count, rows_in, chan_dev, tok_local)
    q, k, v = (got[:, index].reshape(ctx_count * chan_dev, tok_local) for index in range(3))
    gated = long_conv(rank, q, k, v, filters, short_taps, skip_gain)
    gated = gated.reshape(ctx_count, chan_dev, tok_local)
    gated = lax.all_to_all(gated, "ctx", 0, 0, tiled=True).reshape(chan_tp, tok_local)
    parts = project(gated, out_weight, tp_count)
    return combine(lax.all_to_all(parts, "tp", 0, 0, tiled=True))


def solution(mesh):
    placed = (P(None, "tp", "ctx"), P(None, None, "tp"), P("tp", None), P("tp"), P("tp", None))
    return jax.shard_map(
        local, mesh=mesh, in_specs=placed, out_specs=P("tp", "ctx"), check_vma=False
    )
```

```python
import jax
import jax.numpy as jnp
from jax import lax
from jax.experimental import pallas as pl
from jax.experimental.pallas import tpu as pltpu
from jax.sharding import PartitionSpec as P


GROUP = 16
LANES = 128
CHUNK = 1024
CORE_PAIRS = [(0, 1), (1, 0), (2, 3), (3, 2)]
CHIP_PAIRS = [(0, 2), (2, 0), (1, 3), (3, 1)]

f32 = jnp.float32
bf16 = jnp.bfloat16


def params(mib):
    return pltpu.CompilerParams(vmem_limit_bytes=mib << 20)


def table_kernel(rank_ref, filter_ref, table_ref, line_ref):
    seq_len = filter_ref.shape[1]
    own = (rank_ref[0] * 4 // GROUP) % 8
    line_ref[:, :LANES] = jnp.zeros((8, LANES), f32)
    for at in range(0, seq_len, CHUNK):
        piece = filter_ref[:, at : at + CHUNK].astype(f32)
        sub = lax.broadcasted_iota(jnp.int32, piece.shape, 0)
        chosen = jnp.sum(jnp.where(sub == own, piece, 0.0), axis=0, keepdims=True)
        line_ref[:, LANES + at : LANES + at + CHUNK] = jnp.broadcast_to(chosen, piece.shape)
    for at in range(0, seq_len, CHUNK):
        piece = pltpu.roll(line_ref[:, at : at + CHUNK + LANES], 0, 1, stride=1, stride_axis=0)
        for tile in range(LANES // 16):
            upper = pltpu.roll(piece, 16 * tile, 1)[:, LANES:]
            lower = pltpu.roll(piece, 16 * tile + 8, 1)[:, LANES:]
            both = jnp.concatenate([upper, lower], axis=0).astype(bf16)
            for block in range(CHUNK // LANES):
                to_row = (block % 2) * LANES + 16 * tile
                to_col = (at // LANES + block) // 2 * LANES
                table_ref[to_row : to_row + 16, to_col : to_col + LANES] = both[:, block * LANES : (block + 1) * LANES]


def make_table(rank, filters):
    seq_len = filters.shape[1]
    return pl.pallas_call(
        table_kernel,
        out_shape=jax.ShapeDtypeStruct((2 * LANES, seq_len // 2), bf16),
        grid_spec=pltpu.PrefetchScalarGridSpec(
            num_scalar_prefetch=1,
            grid=(1,),
            in_specs=[pl.BlockSpec((8, seq_len), lambda i, r: (r[0] * 4 // GROUP // 8, 0))],
            out_specs=pl.BlockSpec((2 * LANES, seq_len // 2), lambda i, r: (0, 0)),
            scratch_shapes=[pltpu.VMEM((8, LANES + seq_len), f32)],
        ),
        compiler_params=params(16),
        cost_estimate=pl.CostEstimate(flops=1 << 26, bytes_accessed=1 << 23, transcendentals=0),
        name="make_table",
    )(rank, filters)


def pattern(values):
    row = lax.broadcasted_iota(jnp.int32, (8, LANES), 0) % len(values)
    tile = jnp.full((8, LANES), values[-1], f32)
    for index in range(len(values) - 1):
        tile = jnp.where(row == index, values[index], tile)
    return tile


def conv_kernel(rank_ref, value_ref, far_ref, taps_ref, skip_ref, out_ref, pair_ref, sum_ref, table_ref, sems):
    pieces = [
        pltpu.make_async_copy(far_ref.at[:, at : at + CHUNK], table_ref.at[:, at : at + CHUNK], sems.at[at // CHUNK])
        for at in range(0, far_ref.shape[1], CHUNK)
    ]
    for piece in pieces:
        piece.start()
    blocks = value_ref.shape[0]
    rows = blocks * 4
    first = rank_ref[0] * 4
    value = value_ref[...].astype(f32)
    lane = lax.broadcasted_iota(jnp.int32, value.shape, 2)
    sub = lax.broadcasted_iota(jnp.int32, (blocks // 2, 8, LANES), 1)

    def delayed(array):
        return jnp.concatenate([jnp.zeros((1, 8, LANES), f32), array[:-1]], axis=0)

    def tile_of(offset):
        return pattern([taps_ref[offset, feature, first + c] for feature in (1, 2) for c in range(4)])[None]

    conv = tile_of(0) * value
    for offset in (1, 2):
        turned = pltpu.roll(value, offset, 2)
        conv = conv + tile_of(offset) * jnp.where(lane < offset, delayed(turned), turned)
    kv = (conv * pltpu.roll(conv, 4, 1)).astype(bf16).astype(f32)
    kv = kv.reshape(blocks // 2, 2, 8, LANES)
    even, odd = kv[:, 0], kv[:, 1]
    pair_ref[:, :LANES] = jnp.where(sub < 4, even, odd).reshape(rows, LANES).astype(bf16)
    pair_ref[:, LANES:] = jnp.where(sub < 4, delayed(odd), even).reshape(rows, LANES).astype(bf16)

    direct = pattern([skip_ref[first + c] for c in range(4)])[None]
    sum_ref[...] = (pair_ref[:, :LANES].astype(f32).reshape(rows // 8, 8, LANES) * direct).reshape(rows, LANES)
    for part in range(rows // 16):
        begin = part * 16
        if part * 256 % CHUNK == 0:
            pieces[part * 256 // CHUNK].wait()
        moved = jnp.dot(
            pair_ref[: rows - begin, :],
            table_ref[:, part * 256 : part * 256 + 256],
            preferred_element_type=f32,
        )
        sum_ref[begin:, :] += moved[:, :LANES]
        sum_ref[begin + 8 :, :] += moved[: rows - begin - 8, LANES:]
    out_ref[...] = sum_ref[...].astype(bf16)


def long_conv(rank, value, table, short_taps, skip_gain):
    rows = value.shape[0] * 4
    in_vmem = pl.BlockSpec(memory_space=pltpu.VMEM)
    in_smem = pl.BlockSpec(memory_space=pltpu.SMEM)
    return pl.pallas_call(
        conv_kernel,
        out_shape=jax.ShapeDtypeStruct((rows, LANES), bf16),
        in_specs=[in_smem, in_vmem, pl.BlockSpec(memory_space=pltpu.HBM), in_smem, in_smem],
        out_specs=in_vmem,
        scratch_shapes=[
            pltpu.VMEM((rows, 2 * LANES), bf16),
            pltpu.VMEM((rows, LANES), f32),
            pltpu.VMEM(table.shape, bf16),
            pltpu.SemaphoreType.DMA((table.shape[1] // CHUNK,)),
        ],
        compiler_params=params(16),
        cost_estimate=pl.CostEstimate(flops=1 << 31, bytes_accessed=1 << 20, transcendentals=0),
        name="long_conv",
    )(rank, value, table, short_taps, skip_gain)


def turn_kernel(weight_ref, out_ref):
    for at in range(0, weight_ref.shape[1], 256):
        out_ref[at : at + 256, :] = jnp.transpose(weight_ref[:, at : at + 256])


def turn(weight):
    return pl.pallas_call(
        turn_kernel,
        out_shape=jax.ShapeDtypeStruct(weight.shape[::-1], bf16),
        compiler_params=params(16),
        cost_estimate=pl.CostEstimate(flops=1 << 20, bytes_accessed=1 << 22, transcendentals=0),
        name="turn",
    )(weight)


def project_kernel(member_ref, q_ref, q_other_ref, mix_ref, mix_other_ref, weight_ref, weight_other_ref, out_ref):
    gated = (q_ref[...] * mix_ref[...].astype(f32)).astype(bf16)
    gated_other = (q_other_ref[...] * mix_other_ref[...].astype(f32)).astype(bf16)
    total = jnp.dot(weight_ref[...], gated, preferred_element_type=f32)
    total = total + jnp.dot(weight_other_ref[...], gated_other, preferred_element_type=f32)
    out_ref[...] = total.astype(out_ref.dtype)


def project(member, q, q_other, mix, mix_other, weight, weight_other, kind):
    channels, tokens = mix.shape
    whole = pl.BlockSpec((channels, tokens), lambda i, m: (0, 0))
    block = pl.BlockSpec((channels, channels), lambda i, m: (m[0], 0))
    return pl.pallas_call(
        project_kernel,
        out_shape=jax.ShapeDtypeStruct((channels, tokens), kind),
        grid_spec=pltpu.PrefetchScalarGridSpec(
            num_scalar_prefetch=1,
            grid=(1,),
            in_specs=[whole] * 4 + [block] * 2,
            out_specs=whole,
        ),
        compiler_params=params(16),
        cost_estimate=pl.CostEstimate(flops=1 << 27, bytes_accessed=1 << 21, transcendentals=0),
    )(member, q, q_other, mix, mix_other, weight, weight_other)


def local(features, short_taps, filters, skip_gain, out_weight):
    chan_tp, tok_local = features.shape[1:]
    ctx_count = lax.axis_size("ctx")
    chan_dev = chan_tp // ctx_count
    rank = jnp.full((1,), lax.axis_index("ctx"), jnp.int32)
    member = jnp.full((1,), lax.axis_index("tp"), jnp.int32)

    sent = features[1:].reshape(2, ctx_count, chan_dev, tok_local).transpose(1, 0, 2, 3)
    got = lax.all_to_all(sent, "ctx", 0, 0, tiled=True)
    got = got.reshape(ctx_count, 2 * chan_dev, tok_local)
    weight = turn(out_weight)
    weight_other = lax.ppermute(weight, "tp", CORE_PAIRS)
    table = make_table(rank, filters)

    mix = long_conv(rank, got, table, short_taps, skip_gain).reshape(ctx_count, chan_dev, tok_local)
    mix, late, late_taps = lax.optimization_barrier((mix, features, short_taps))
    mix = lax.all_to_all(mix, "ctx", 0, 0, tiled=True).reshape(chan_tp, tok_local)
    halo = lax.ppermute(late[0, :, tok_local - 2 :], "ctx", [(i, i + 1) for i in range(ctx_count - 1)])
    extended = jnp.concatenate([halo, late[0]], axis=1).astype(f32)
    q = sum(late_taps[j, 0][:, None] * extended[:, 2 - j : 2 - j + tok_local] for j in range(3))
    q_other = lax.ppermute(q, "tp", CORE_PAIRS)
    mix_other = lax.ppermute(mix, "tp", CORE_PAIRS)
    operands = (q, q_other, mix, mix_other, weight, weight_other)
    away = project(lax.bitwise_xor(member, 2), *operands, bf16)
    arrived = lax.ppermute(away, "tp", CHIP_PAIRS)
    home = project(member, *operands, f32)
    return (home + arrived.astype(f32)).astype(bf16)


def solution(mesh):
    placed = (P(None, "tp", "ctx"), P(None, None, "tp"), P("tp", None), P("tp"), P("tp", None))
    return jax.shard_map(
        local, mesh=mesh, in_specs=placed, out_specs=P("tp", "ctx"), check_vma=False
    )
```

```python
import jax
import jax.numpy as jnp
from jax import lax
from jax.experimental import pallas as pl
from jax.experimental.pallas import tpu as pltpu
from jax.sharding import PartitionSpec as P


GROUP = 16
LANES = 128
CHUNK = 1024
TABLE_STEPS = 4
LEAD = 48
CORE_PAIRS = [(0, 1), (1, 0), (2, 3), (3, 2)]
CHIP_PAIRS = [(0, 2), (2, 0), (1, 3), (3, 1)]

f32 = jnp.float32
bf16 = jnp.bfloat16


def params(mib):
    return pltpu.CompilerParams(vmem_limit_bytes=mib << 20)


def table_kernel(rank_ref, filter_ref, table_ref, line_ref):
    length = filter_ref.shape[1]
    own = (rank_ref[0] * 4 // GROUP) % 8

    @pl.when(pl.program_id(0) == 0)
    def _():
        line_ref[:, :LANES] = jnp.zeros((8, LANES), f32)

    @pl.when(pl.program_id(0) > 0)
    def _():
        line_ref[:, :LANES] = line_ref[:, length:]

    for at in range(0, length, CHUNK):
        piece = filter_ref[:, at : at + CHUNK].astype(f32)
        sub = lax.broadcasted_iota(jnp.int32, piece.shape, 0)
        chosen = jnp.sum(jnp.where(sub == own, piece, 0.0), axis=0, keepdims=True)
        line_ref[:, LANES + at : LANES + at + CHUNK] = jnp.broadcast_to(chosen, piece.shape)
    for at in range(0, length, CHUNK):
        piece = pltpu.roll(line_ref[:, at : at + CHUNK + LANES], 0, 1, stride=1, stride_axis=0)
        for tile in range(LANES // 16):
            upper = pltpu.roll(piece, 16 * tile, 1)[:, LANES:]
            lower = pltpu.roll(piece, 16 * tile + 8, 1)[:, LANES:]
            both = jnp.concatenate([upper, lower], axis=0).astype(bf16)
            for block in range(CHUNK // LANES):
                to_row = (block % 2) * LANES + 16 * tile
                to_col = (at // LANES + block) // 2 * LANES
                table_ref[to_row : to_row + 16, to_col : to_col + LANES] = both[:, block * LANES : (block + 1) * LANES]


def make_table(rank, filters):
    seq_len = filters.shape[1]
    length = seq_len // TABLE_STEPS
    return pl.pallas_call(
        table_kernel,
        out_shape=jax.ShapeDtypeStruct((2 * LANES, seq_len // 2), bf16),
        grid_spec=pltpu.PrefetchScalarGridSpec(
            num_scalar_prefetch=1,
            grid=(TABLE_STEPS,),
            in_specs=[pl.BlockSpec((8, length), lambda i, r: (r[0] * 4 // GROUP // 8, i))],
            out_specs=pl.BlockSpec((2 * LANES, length // 2), lambda i, r: (0, i)),
            scratch_shapes=[pltpu.VMEM((8, LANES + length), f32)],
        ),
        compiler_params=params(60),
        cost_estimate=pl.CostEstimate(flops=1 << 26, bytes_accessed=1 << 23, transcendentals=0),
        name="make_table",
    )(rank, filters)


def pattern(values):
    row = lax.broadcasted_iota(jnp.int32, (8, LANES), 0) % len(values)
    tile = jnp.full((8, LANES), values[-1], f32)
    for index in range(len(values) - 1):
        tile = jnp.where(row == index, values[index], tile)
    return tile


def conv_kernel(rank_ref, value_ref, far_ref, taps_ref, skip_ref, out_ref, pair_ref, sum_ref, table_ref, sems):
    pieces = [
        pltpu.make_async_copy(far_ref.at[:, at : at + CHUNK], table_ref.at[:, at : at + CHUNK], sems.at[at // CHUNK])
        for at in range(0, far_ref.shape[1], CHUNK)
    ]
    for piece in pieces:
        piece.start()
    blocks = value_ref.shape[0]
    rows = blocks * 4
    first = rank_ref[0] * 4
    value = value_ref[...].astype(f32)
    lane = lax.broadcasted_iota(jnp.int32, value.shape, 2)
    sub = lax.broadcasted_iota(jnp.int32, (blocks // 2, 8, LANES), 1)

    def delayed(array):
        return jnp.concatenate([jnp.zeros((1, 8, LANES), f32), array[:-1]], axis=0)

    def tile_of(offset):
        return pattern([taps_ref[offset, feature, first + c] for feature in (1, 2) for c in range(4)])[None]

    conv = tile_of(0) * value
    for offset in (1, 2):
        turned = pltpu.roll(value, offset, 2)
        conv = conv + tile_of(offset) * jnp.where(lane < offset, delayed(turned), turned)
    kv = (conv * pltpu.roll(conv, 4, 1)).astype(bf16).astype(f32)
    kv = kv.reshape(blocks // 2, 2, 8, LANES)
    even, odd = kv[:, 0], kv[:, 1]
    pair_ref[:LEAD, :] = jnp.zeros((LEAD, 2 * LANES), bf16)
    pair_ref[LEAD:, :LANES] = jnp.where(sub < 4, even, odd).reshape(rows, LANES).astype(bf16)
    pair_ref[LEAD:, LANES:] = jnp.where(sub < 4, delayed(odd), even).reshape(rows, LANES).astype(bf16)

    direct = pattern([skip_ref[first + c] for c in range(4)])[None]
    sum_ref[...] = (pair_ref[LEAD:, :LANES].astype(f32).reshape(rows // 8, 8, LANES) * direct).reshape(rows, LANES)
    for index, piece in enumerate(pieces):
        begin = 64 * index
        piece.wait()
        left = [pair_ref[LEAD - 16 * s : LEAD - 16 * s + rows - begin, :] for s in range(4)]
        right = [table_ref[:, index * CHUNK + 256 * s : index * CHUNK + 256 * (s + 1)] for s in range(4)]
        moved = jnp.dot(
            jnp.concatenate(left, axis=1), jnp.concatenate(right, axis=0), preferred_element_type=f32
        )
        sum_ref[begin:, :] += moved[:, :LANES]
        sum_ref[begin + 8 :, :] += moved[: rows - begin - 8, LANES:]
    out_ref[...] = sum_ref[...].astype(bf16)


def long_conv(rank, value, table, short_taps, skip_gain):
    rows = value.shape[0] * 4
    in_vmem = pl.BlockSpec(memory_space=pltpu.VMEM)
    in_smem = pl.BlockSpec(memory_space=pltpu.SMEM)
    return pl.pallas_call(
        conv_kernel,
        out_shape=jax.ShapeDtypeStruct((rows, LANES), bf16),
        in_specs=[in_smem, in_vmem, pl.BlockSpec(memory_space=pltpu.HBM), in_smem, in_smem],
        out_specs=in_vmem,
        scratch_shapes=[
            pltpu.VMEM((LEAD + rows, 2 * LANES), bf16),
            pltpu.VMEM((rows, LANES), f32),
            pltpu.VMEM(table.shape, bf16),
            pltpu.SemaphoreType.DMA((table.shape[1] // CHUNK,)),
        ],
        compiler_params=params(16),
        cost_estimate=pl.CostEstimate(flops=1 << 31, bytes_accessed=1 << 20, transcendentals=0),
        name="long_conv",
    )(rank, value, table, short_taps, skip_gain)


def turn_kernel(core_ref, weight_ref, out_ref):
    out_ref[...] = jnp.transpose(weight_ref[...])


def turn(core, weight):
    width = weight.shape[0]
    return pl.pallas_call(
        turn_kernel,
        out_shape=jax.ShapeDtypeStruct((weight.shape[1] // 2, width), bf16),
        grid_spec=pltpu.PrefetchScalarGridSpec(
            num_scalar_prefetch=1,
            grid=(2,),
            in_specs=[pl.BlockSpec((width, width), lambda i, c: (0, 2 * i + c[0]))],
            out_specs=pl.BlockSpec((width, width), lambda i, c: (i, 0)),
        ),
        compiler_params=params(16),
        cost_estimate=pl.CostEstimate(flops=1 << 20, bytes_accessed=1 << 21, transcendentals=0),
        name="turn",
    )(core, weight)


def edge_kernel(rows_ref, out_ref):
    out_ref[...] = jnp.transpose(rows_ref[0])[LANES - 16 :, :]


def edge(features):
    channels, tokens = features.shape[1:]
    return pl.pallas_call(
        edge_kernel,
        out_shape=jax.ShapeDtypeStruct((16, channels), bf16),
        grid=(1,),
        in_specs=[pl.BlockSpec((1, channels, tokens), lambda i: (0, 0, 0))],
        out_specs=pl.BlockSpec((16, channels), lambda i: (0, 0)),
        compiler_params=params(16),
        cost_estimate=pl.CostEstimate(flops=1 << 16, bytes_accessed=1 << 17, transcendentals=0),
        name="edge",
    )(features)


def query_kernel(rows_ref, halo_ref, taps_ref, out_ref):
    value = rows_ref[0].astype(f32)
    lane = lax.broadcasted_iota(jnp.int32, value.shape, 1)
    halo = jnp.transpose(halo_ref[...].astype(f32))
    taps = taps_ref[:, 0, :]
    taps = jnp.transpose(jnp.concatenate([taps, jnp.zeros((5, taps.shape[1]), f32)], axis=0))
    once = jnp.where(lane == 0, halo[:, 15:16], pltpu.roll(value, 1, 1))
    twice = jnp.where(lane == 0, halo[:, 14:15], jnp.where(lane == 1, halo[:, 15:16], pltpu.roll(value, 2, 1)))
    out_ref[...] = taps[:, 0:1] * value + taps[:, 1:2] * once + taps[:, 2:3] * twice


def query_conv(features, halo, short_taps):
    channels, tokens = features.shape[1:]
    return pl.pallas_call(
        query_kernel,
        out_shape=jax.ShapeDtypeStruct((channels, tokens), f32),
        grid=(1,),
        in_specs=[
            pl.BlockSpec((1, channels, tokens), lambda i: (0, 0, 0)),
            pl.BlockSpec(halo.shape, lambda i: (0, 0)),
            pl.BlockSpec(short_taps.shape, lambda i: (0, 0, 0)),
        ],
        out_specs=pl.BlockSpec((channels, tokens), lambda i: (0, 0)),
        compiler_params=params(16),
        cost_estimate=pl.CostEstimate(flops=1 << 20, bytes_accessed=1 << 19, transcendentals=0),
        name="query_conv",
    )(features, halo, short_taps)


def project_kernel(chip_ref, q_ref, q_other_ref, mix_ref, mix_other_ref, weight_ref, weight_other_ref, out_ref):
    width = out_ref.shape[0]
    block = pl.ds(pl.multiple_of(chip_ref[0] * width, width), width)
    gated = (q_ref[...] * mix_ref[...].astype(f32)).astype(bf16)
    gated_other = (q_other_ref[...] * mix_other_ref[...].astype(f32)).astype(bf16)
    total = jnp.dot(weight_ref[block, :], gated, preferred_element_type=f32)
    total = total + jnp.dot(weight_other_ref[block, :], gated_other, preferred_element_type=f32)
    out_ref[...] = total.astype(out_ref.dtype)


def project(chip, q, q_other, mix, mix_other, weight, weight_other, kind):
    in_vmem = pl.BlockSpec(memory_space=pltpu.VMEM)
    return pl.pallas_call(
        project_kernel,
        out_shape=jax.ShapeDtypeStruct(mix.shape, kind),
        in_specs=[pl.BlockSpec(memory_space=pltpu.SMEM)] + [in_vmem] * 6,
        out_specs=in_vmem,
        compiler_params=params(16),
        cost_estimate=pl.CostEstimate(flops=1 << 27, bytes_accessed=1 << 21, transcendentals=0),
    )(chip, q, q_other, mix, mix_other, weight, weight_other)


def local(features, short_taps, filters, skip_gain, out_weight):
    chan_tp, tok_local = features.shape[1:]
    ctx_count = lax.axis_size("ctx")
    chan_dev = chan_tp // ctx_count
    rank = jnp.full((1,), lax.axis_index("ctx"), jnp.int32)
    chip = jnp.full((1,), lax.axis_index("tp") // 2, jnp.int32)
    core = jnp.full((1,), lax.axis_index("tp") % 2, jnp.int32)

    sent = features[1:].reshape(2, ctx_count, chan_dev, tok_local).transpose(1, 0, 2, 3)
    got = lax.all_to_all(sent, "ctx", 0, 0, tiled=True)
    got = got.reshape(ctx_count, 2 * chan_dev, tok_local)
    weight_given = turn(1 - core, out_weight)
    table = pltpu.with_memory_space_constraint(make_table(rank, filters), pltpu.HBM)
    last = edge(features)
    halo = lax.ppermute(last, "ctx", [(i, i + 1) for i in range(ctx_count - 1)])
    weight_other = lax.ppermute(weight_given, "tp", CORE_PAIRS)

    mix = long_conv(rank, got, table, short_taps, skip_gain).reshape(ctx_count, chan_dev, tok_local)
    mix = lax.all_to_all(mix, "ctx", 0, 0, tiled=True).reshape(chan_tp, tok_local)
    weight = turn(core, out_weight)
    q = query_conv(features, halo, short_taps)
    q_other = lax.ppermute(q, "tp", CORE_PAIRS)
    mix_other = lax.ppermute(mix, "tp", CORE_PAIRS)
    operands = (q, q_other, mix, mix_other, weight, weight_other)
    away = project(1 - chip, *operands, bf16)
    arrived = lax.ppermute(away, "tp", CHIP_PAIRS)
    home = project(chip, *operands, f32)
    return (home + arrived.astype(f32)).astype(bf16)


def solution(mesh):
    placed = (P(None, "tp", "ctx"), P(None, None, "tp"), P("tp", None), P("tp"), P("tp", None))
    return jax.shard_map(
        local, mesh=mesh, in_specs=placed, out_specs=P("tp", "ctx"), check_vma=False
    )
```

```python
import jax
import jax.numpy as jnp
from jax import lax
from jax.experimental import pallas as pl
from jax.experimental.pallas import tpu as pltpu
from jax.sharding import PartitionSpec as P


GROUP = 16
LANES = 128
CHUNK = 1024
LEAD = 48
CORE_PAIRS = [(0, 1), (1, 0), (2, 3), (3, 2)]
CHIP_PAIRS = [(0, 2), (2, 0), (1, 3), (3, 1)]

f32 = jnp.float32
bf16 = jnp.bfloat16


def params(mib):
    return pltpu.CompilerParams(vmem_limit_bytes=mib << 20)


def in_hbm(array):
    return pltpu.with_memory_space_constraint(array, pltpu.HBM)


def load_line(filter_ref, own, line_ref):
    line_ref[:, :LANES] = jnp.zeros((8, LANES), f32)
    for at in range(0, filter_ref.shape[1], CHUNK):
        piece = filter_ref[:, at : at + CHUNK].astype(f32)
        sub = lax.broadcasted_iota(jnp.int32, piece.shape, 0)
        chosen = jnp.sum(jnp.where(sub == own, piece, 0.0), axis=0, keepdims=True)
        line_ref[:, LANES + at : LANES + at + CHUNK] = jnp.broadcast_to(chosen, piece.shape)


def fill_table(line_ref, table_ref, at):
    piece = line_ref[:, at : at + CHUNK + LANES]
    piece = jnp.concatenate([pltpu.roll(piece, first, 1, stride=1, stride_axis=0) for first in (0, 8)], axis=0).astype(bf16)
    for tile in range(LANES // 16):
        moved = pltpu.roll(piece, 16 * tile, 1)[:, LANES:] if tile else piece[:, LANES:]
        for block in range(CHUNK // LANES):
            to_row = (block % 2) * LANES + 16 * tile
            to_col = (at // LANES + block) // 2 * LANES
            table_ref[to_row : to_row + 16, to_col : to_col + LANES] = moved[:, block * LANES : (block + 1) * LANES]


def pattern(values):
    row = lax.broadcasted_iota(jnp.int32, (8, LANES), 0) % len(values)
    tile = jnp.full((8, LANES), values[-1], f32)
    for index in range(len(values) - 1):
        tile = jnp.where(row == index, values[index], tile)
    return tile


def conv_kernel(rank_ref, value_ref, filter_ref, taps_ref, skip_ref, out_ref, pair_ref, sum_ref, line_ref, table_ref):
    load_line(filter_ref, (rank_ref[0] * 4 // GROUP) % 8, line_ref)
    blocks = value_ref.shape[0]
    rows = blocks * 4
    first = rank_ref[0] * 4
    value = value_ref[...].astype(f32)
    lane = lax.broadcasted_iota(jnp.int32, value.shape, 2)
    sub = lax.broadcasted_iota(jnp.int32, (blocks // 2, 8, LANES), 1)

    def delayed(array):
        return jnp.concatenate([jnp.zeros((1, 8, LANES), f32), array[:-1]], axis=0)

    def tile_of(offset):
        return pattern([taps_ref[offset, feature, first + c] for feature in (1, 2) for c in range(4)])[None]

    conv = tile_of(0) * value
    for offset in (1, 2):
        turned = pltpu.roll(value, offset, 2)
        conv = conv + tile_of(offset) * jnp.where(lane < offset, delayed(turned), turned)
    kv = (conv * pltpu.roll(conv, 4, 1)).astype(bf16).astype(f32)
    kv = kv.reshape(blocks // 2, 2, 8, LANES)
    even, odd = kv[:, 0], kv[:, 1]
    pair_ref[:LEAD, :] = jnp.zeros((LEAD, 2 * LANES), bf16)
    pair_ref[LEAD:, :LANES] = jnp.where(sub < 4, even, odd).reshape(rows, LANES).astype(bf16)
    pair_ref[LEAD:, LANES:] = jnp.where(sub < 4, delayed(odd), even).reshape(rows, LANES).astype(bf16)

    direct = pattern([skip_ref[first + c] for c in range(4)])[None]
    sum_ref[...] = (pair_ref[LEAD:, :LANES].astype(f32).reshape(rows // 8, 8, LANES) * direct).reshape(rows, LANES)
    for index in range(rows // 64):
        begin, base = 64 * index, CHUNK * index
        for at in (2 * base, 2 * base + CHUNK):
            fill_table(line_ref, table_ref, at)
        left = [pair_ref[LEAD - 16 * s : LEAD - 16 * s + rows - begin, :] for s in range(4)]
        right = [table_ref[:, base + 256 * s : base + 256 * (s + 1)] for s in range(4)]
        moved = jnp.dot(
            jnp.concatenate(left, axis=1), jnp.concatenate(right, axis=0), preferred_element_type=f32
        )
        sum_ref[begin:, :] += moved[:, :LANES]
        sum_ref[begin + 8 :, :] += moved[: rows - begin - 8, LANES:]
    out_ref[...] = sum_ref[...].astype(bf16)


def long_conv(rank, value, filters, short_taps, skip_gain):
    blocks = value.shape[0]
    rows = blocks * 4
    seq_len = filters.shape[1]
    in_smem = pl.BlockSpec(memory_space=pltpu.SMEM)
    return pl.pallas_call(
        conv_kernel,
        out_shape=jax.ShapeDtypeStruct((rows, LANES), bf16),
        grid_spec=pltpu.PrefetchScalarGridSpec(
            num_scalar_prefetch=1,
            grid=(1,),
            in_specs=[
                pl.BlockSpec(value.shape, lambda i, r: (0, 0, 0)),
                pl.BlockSpec((8, seq_len), lambda i, r: (r[0] * 4 // GROUP // 8, 0)),
                in_smem,
                in_smem,
            ],
            out_specs=pl.BlockSpec((rows, LANES), lambda i, r: (0, 0)),
            scratch_shapes=[
                pltpu.VMEM((LEAD + rows, 2 * LANES), bf16),
                pltpu.VMEM((rows, LANES), f32),
                pltpu.VMEM((8, LANES + seq_len), f32),
                pltpu.VMEM((2 * LANES, seq_len // 2), bf16),
            ],
        ),
        compiler_params=params(16),
        cost_estimate=pl.CostEstimate(flops=1 << 31, bytes_accessed=1 << 20, transcendentals=0),
        name="long_conv",
    )(rank, value, filters, short_taps, skip_gain)


def turn_kernel(weight_ref, out_ref):
    out_ref[...] = jnp.transpose(weight_ref[...])


def turn(weight):
    width, total = weight.shape
    return pl.pallas_call(
        turn_kernel,
        out_shape=jax.ShapeDtypeStruct((total, width), bf16),
        grid=(total // width,),
        in_specs=[pl.BlockSpec((width, width), lambda i: (0, i))],
        out_specs=pl.BlockSpec((width, width), lambda i: (i, 0)),
        compiler_params=params(16),
        cost_estimate=pl.CostEstimate(flops=1 << 20, bytes_accessed=1 << 22, transcendentals=0),
        name="turn",
    )(weight)


def edge_kernel(rows_ref, out_ref):
    out_ref[...] = jnp.transpose(rows_ref[0])[LANES - 16 :, :]


def edge(features):
    channels, tokens = features.shape[1:]
    return pl.pallas_call(
        edge_kernel,
        out_shape=jax.ShapeDtypeStruct((16, channels), bf16),
        grid=(1,),
        in_specs=[pl.BlockSpec((1, channels, tokens), lambda i: (0, 0, 0))],
        out_specs=pl.BlockSpec((16, channels), lambda i: (0, 0)),
        compiler_params=params(16),
        cost_estimate=pl.CostEstimate(flops=1 << 16, bytes_accessed=1 << 17, transcendentals=0),
        name="edge",
    )(features)


def query_kernel(rows_ref, halo_ref, taps_ref, out_ref):
    value = rows_ref[0].astype(f32)
    lane = lax.broadcasted_iota(jnp.int32, value.shape, 1)
    halo = jnp.transpose(halo_ref[...].astype(f32))
    taps = taps_ref[:, 0, :]
    taps = jnp.transpose(jnp.concatenate([taps, jnp.zeros((5, taps.shape[1]), f32)], axis=0))
    once = jnp.where(lane == 0, halo[:, 15:16], pltpu.roll(value, 1, 1))
    twice = jnp.where(lane == 0, halo[:, 14:15], jnp.where(lane == 1, halo[:, 15:16], pltpu.roll(value, 2, 1)))
    out_ref[...] = taps[:, 0:1] * value + taps[:, 1:2] * once + taps[:, 2:3] * twice


def query_conv(features, halo, short_taps):
    channels, tokens = features.shape[1:]
    return pl.pallas_call(
        query_kernel,
        out_shape=jax.ShapeDtypeStruct((channels, tokens), f32),
        grid=(1,),
        in_specs=[
            pl.BlockSpec((1, channels, tokens), lambda i: (0, 0, 0)),
            pl.BlockSpec(halo.shape, lambda i: (0, 0)),
            pl.BlockSpec(short_taps.shape, lambda i: (0, 0, 0)),
        ],
        out_specs=pl.BlockSpec((channels, tokens), lambda i: (0, 0)),
        compiler_params=params(16),
        cost_estimate=pl.CostEstimate(flops=1 << 20, bytes_accessed=1 << 19, transcendentals=0),
        name="query_conv",
    )(features, halo, short_taps)


def gated_of(q_ref, mix_ref):
    return (q_ref[...] * mix_ref[...].astype(f32)).astype(bf16)


def give_kernel(member_ref, q_ref, mix_ref, weight_ref, out_ref):
    gated = gated_of(q_ref, mix_ref)
    width = mix_ref.shape[0]
    for chip in range(2):
        at = (2 * chip + 1 - member_ref[0] % 2) * width
        out_ref[chip * width : (chip + 1) * width, :] = jnp.dot(
            weight_ref[pl.ds(pl.multiple_of(at, width), width), :], gated, preferred_element_type=f32
        ).astype(bf16)


def keep_kernel(member_ref, q_ref, mix_ref, weight_ref, given_ref, out_ref):
    gated = gated_of(q_ref, mix_ref)
    width = mix_ref.shape[0]
    at = pl.multiple_of(member_ref[0] * width, width)
    chip = pl.multiple_of(member_ref[0] // 2 * width, width)
    own = jnp.dot(weight_ref[pl.ds(at, width), :], gated, preferred_element_type=f32)
    out_ref[...] = (own + given_ref[pl.ds(chip, width), :].astype(f32)).astype(out_ref.dtype)


def project(kernel, member, operands, rows, kind):
    in_vmem = pl.BlockSpec(memory_space=pltpu.VMEM)
    return pl.pallas_call(
        kernel,
        out_shape=jax.ShapeDtypeStruct((rows, operands[1].shape[1]), kind),
        in_specs=[pl.BlockSpec(memory_space=pltpu.SMEM)] + [in_vmem] * len(operands),
        out_specs=in_vmem,
        compiler_params=params(16),
        cost_estimate=pl.CostEstimate(flops=1 << 27, bytes_accessed=1 << 21, transcendentals=0),
    )(member, *operands)


def local(features, short_taps, filters, skip_gain, out_weight):
    chan_tp, tok_local = features.shape[1:]
    ctx_count = lax.axis_size("ctx")
    chan_dev = chan_tp // ctx_count
    rank = jnp.full((1,), lax.axis_index("ctx"), jnp.int32)
    member = jnp.full((1,), lax.axis_index("tp"), jnp.int32)

    sent = features[1:].reshape(2, ctx_count, chan_dev, tok_local).transpose(1, 0, 2, 3)
    got = lax.all_to_all(sent, "ctx", 0, 0, tiled=True)
    got = got.reshape(ctx_count, 2 * chan_dev, tok_local)
    last = edge(in_hbm(features))
    halo = lax.ppermute(last, "ctx", [(i, i + 1) for i in range(ctx_count - 1)])
    mix = long_conv(rank, got, *map(in_hbm, (filters, short_taps, skip_gain))).reshape(ctx_count, chan_dev, tok_local)
    mix = lax.all_to_all(mix, "ctx", 0, 0, tiled=True).reshape(chan_tp, tok_local)
    q = query_conv(features, halo, short_taps)
    weight = turn(in_hbm(out_weight))
    given = project(give_kernel, member, (q, mix, weight), 2 * chan_tp, bf16)
    given = lax.ppermute(given, "tp", CORE_PAIRS)
    operands = (q, mix, weight, given)
    away = project(keep_kernel, lax.bitwise_xor(member, 2), operands, chan_tp, bf16)
    arrived = lax.ppermute(away, "tp", CHIP_PAIRS)
    home = project(keep_kernel, member, operands, chan_tp, f32)
    return (home + arrived.astype(f32)).astype(bf16)


def solution(mesh):
    placed = (P(None, "tp", "ctx"), P(None, None, "tp"), P("tp", None), P("tp"), P("tp", None))
    return jax.shard_map(
        local, mesh=mesh, in_specs=placed, out_specs=P("tp", "ctx"), check_vma=False
    )
```

```python
import jax
import jax.numpy as jnp
from jax import lax
from jax.experimental import pallas as pl
from jax.experimental.pallas import tpu as pltpu
from jax.sharding import PartitionSpec as P


GROUP = 16
LANES = 128
CHUNK = 1024
LEAD = 48
CORE_PAIRS = [(0, 1), (1, 0), (2, 3), (3, 2)]
CHIP_PAIRS = [(0, 2), (2, 0), (1, 3), (3, 1)]

f32 = jnp.float32
bf16 = jnp.bfloat16


def params(mib):
    return pltpu.CompilerParams(vmem_limit_bytes=mib << 20)


def in_hbm(array):
    return pltpu.with_memory_space_constraint(array, pltpu.HBM)


def fill_table(line_ref, table_ref, at):
    piece = line_ref[:, at : at + CHUNK + LANES]
    for tile in range(LANES // 16):
        moved = pltpu.roll(piece, 16 * tile, 1)[:, LANES:] if tile else piece[:, LANES:]
        for block in range(CHUNK // LANES):
            to_row = (block % 2) * LANES + 16 * tile
            to_col = (at // LANES + block) // 2 * LANES
            table_ref[to_row : to_row + 16, to_col : to_col + LANES] = moved[:, block * LANES : (block + 1) * LANES]


def pattern(values):
    row = lax.broadcasted_iota(jnp.int32, (8, LANES), 0) % len(values)
    tile = jnp.full((8, LANES), values[-1], f32)
    for index in range(len(values) - 1):
        tile = jnp.where(row == index, values[index], tile)
    return tile


def prepare_kernel(rank_ref, filter_ref, taps_ref, skip_ref, line_ref, tiles_ref, wide_ref):
    own = (rank_ref[0] * 4 // GROUP) % 8
    first = rank_ref[0] * 4
    wide_ref[:, : 2 * LANES] = jnp.zeros((8, 2 * LANES), f32)
    line_ref[:, :LANES] = jnp.zeros((16, LANES), bf16)
    for at in range(0, filter_ref.shape[1], CHUNK):
        piece = filter_ref[:, at : at + CHUNK].astype(f32)
        sub = lax.broadcasted_iota(jnp.int32, piece.shape, 0)
        chosen = jnp.sum(jnp.where(sub == own, piece, 0.0), axis=0, keepdims=True)
        wide_ref[:, 2 * LANES + at : 2 * LANES + at + CHUNK] = jnp.broadcast_to(chosen, piece.shape)
    for at in range(0, filter_ref.shape[1], CHUNK):
        piece = wide_ref[:, LANES + at : 2 * LANES + at + CHUNK]
        both = [pltpu.roll(piece, begin, 1, stride=1, stride_axis=0)[:, LANES:] for begin in (0, 8)]
        line_ref[:, LANES + at : LANES + at + CHUNK] = jnp.concatenate(both, axis=0).astype(bf16)
    for offset in range(3):
        tiles_ref[offset] = pattern([taps_ref[offset, feature, first + c] for feature in (1, 2) for c in range(4)])
    tiles_ref[3] = pattern([skip_ref[first + c] for c in range(4)])


def prepare(rank, filters, short_taps, skip_gain):
    seq_len = filters.shape[1]
    in_smem = pl.BlockSpec(memory_space=pltpu.SMEM)
    return pl.pallas_call(
        prepare_kernel,
        out_shape=[
            jax.ShapeDtypeStruct((16, LANES + seq_len), bf16),
            jax.ShapeDtypeStruct((4, 8, LANES), f32),
        ],
        grid_spec=pltpu.PrefetchScalarGridSpec(
            num_scalar_prefetch=1,
            grid=(1,),
            in_specs=[pl.BlockSpec((8, seq_len), lambda i, r: (r[0] * 4 // GROUP // 8, 0)), in_smem, in_smem],
            out_specs=[
                pl.BlockSpec((16, LANES + seq_len), lambda i, r: (0, 0)),
                pl.BlockSpec((4, 8, LANES), lambda i, r: (0, 0, 0)),
            ],
            scratch_shapes=[pltpu.VMEM((8, 2 * LANES + seq_len), f32)],
        ),
        compiler_params=params(16),
        cost_estimate=pl.CostEstimate(flops=1 << 22, bytes_accessed=1 << 20, transcendentals=0),
        name="prepare",
    )(rank, filters, short_taps, skip_gain)


def pack_kernel(k_ref, v_ref, out_ref):
    rows = k_ref.shape[1]
    k = k_ref[0].astype(f32).reshape(rows // 8, 8, LANES)
    v = v_ref[0].astype(f32).reshape(rows // 8, 8, LANES)
    upper = lax.broadcasted_iota(jnp.int32, k.shape, 1) < 4
    even = jnp.where(upper, k, pltpu.roll(v, 4, 1))
    odd = jnp.where(upper, pltpu.roll(k, 4, 1), v)
    out_ref[...] = jnp.stack([even, odd], axis=1).reshape(rows // 4, 8, LANES).astype(bf16)


def pack(features):
    rows = features.shape[1]
    return pl.pallas_call(
        pack_kernel,
        out_shape=jax.ShapeDtypeStruct((rows // 4, 8, LANES), bf16),
        grid=(1,),
        in_specs=[
            pl.BlockSpec((1, rows, LANES), lambda i: (1, 0, 0)),
            pl.BlockSpec((1, rows, LANES), lambda i: (2, 0, 0)),
        ],
        out_specs=pl.BlockSpec((rows // 4, 8, LANES), lambda i: (0, 0, 0)),
        compiler_params=params(16),
        cost_estimate=pl.CostEstimate(flops=1 << 18, bytes_accessed=1 << 19, transcendentals=0),
        name="pack",
    )(features, features)


def conv_kernel(value_ref, line_ref, tiles_ref, out_ref, pair_ref, sum_ref, table_ref):
    blocks = value_ref.shape[0]
    rows = blocks * 4
    value = value_ref[...].astype(f32)
    lane = lax.broadcasted_iota(jnp.int32, value.shape, 2)
    sub = lax.broadcasted_iota(jnp.int32, (blocks // 2, 8, LANES), 1)

    def delayed(array):
        return jnp.concatenate([jnp.zeros((1, 8, LANES), f32), array[:-1]], axis=0)

    conv = tiles_ref[0][None] * value
    for offset in (1, 2):
        turned = pltpu.roll(value, offset, 2)
        conv = conv + tiles_ref[offset][None] * jnp.where(lane < offset, delayed(turned), turned)
    kv = (conv * pltpu.roll(conv, 4, 1)).astype(bf16).astype(f32)
    kv = kv.reshape(blocks // 2, 2, 8, LANES)
    even, odd = kv[:, 0], kv[:, 1]
    pair_ref[:LEAD, :] = jnp.zeros((LEAD, 2 * LANES), bf16)
    pair_ref[LEAD:, :LANES] = jnp.where(sub < 4, even, odd).reshape(rows, LANES).astype(bf16)
    pair_ref[LEAD:, LANES:] = jnp.where(sub < 4, delayed(odd), even).reshape(rows, LANES).astype(bf16)

    direct = tiles_ref[3][None]
    sum_ref[...] = (pair_ref[LEAD:, :LANES].astype(f32).reshape(rows // 8, 8, LANES) * direct).reshape(rows, LANES)
    for index in range(rows // 64):
        begin, base = 64 * index, CHUNK * index
        for at in (2 * base, 2 * base + CHUNK):
            fill_table(line_ref, table_ref, at)
        left = [pair_ref[LEAD - 16 * s : LEAD - 16 * s + rows - begin, :] for s in range(4)]
        right = [table_ref[:, base + 256 * s : base + 256 * (s + 1)] for s in range(4)]
        moved = jnp.dot(
            jnp.concatenate(left, axis=1), jnp.concatenate(right, axis=0), preferred_element_type=f32
        )
        sum_ref[begin:, :] += moved[:, :LANES]
        sum_ref[begin + 8 :, :] += moved[: rows - begin - 8, LANES:]
    out_ref[...] = sum_ref[...].astype(bf16)


def long_conv(value, line, tiles):
    rows = value.shape[0] * 4
    seq_len = line.shape[1] - LANES
    in_vmem = pl.BlockSpec(memory_space=pltpu.VMEM)
    return pl.pallas_call(
        conv_kernel,
        out_shape=jax.ShapeDtypeStruct((rows, LANES), bf16),
        in_specs=[in_vmem] * 3,
        out_specs=in_vmem,
        scratch_shapes=[
            pltpu.VMEM((LEAD + rows, 2 * LANES), bf16),
            pltpu.VMEM((rows, LANES), f32),
            pltpu.VMEM((2 * LANES, seq_len // 2), bf16),
        ],
        compiler_params=params(16),
        cost_estimate=pl.CostEstimate(flops=1 << 31, bytes_accessed=1 << 20, transcendentals=0),
        name="long_conv",
    )(value, line, tiles)


def turn_kernel(weight_ref, out_ref):
    out_ref[...] = jnp.transpose(weight_ref[...])


def turn(weight):
    width, total = weight.shape
    return pl.pallas_call(
        turn_kernel,
        out_shape=jax.ShapeDtypeStruct((total, width), bf16),
        grid=(total // width,),
        in_specs=[pl.BlockSpec((width, width), lambda i: (0, i))],
        out_specs=pl.BlockSpec((width, width), lambda i: (i, 0)),
        compiler_params=params(16),
        cost_estimate=pl.CostEstimate(flops=1 << 20, bytes_accessed=1 << 22, transcendentals=0),
        name="turn",
    )(weight)


def edge_kernel(rows_ref, out_ref):
    out_ref[...] = jnp.transpose(rows_ref[0])[LANES - 16 :, :]


def edge(features):
    channels, tokens = features.shape[1:]
    return pl.pallas_call(
        edge_kernel,
        out_shape=jax.ShapeDtypeStruct((16, channels), bf16),
        grid=(1,),
        in_specs=[pl.BlockSpec((1, channels, tokens), lambda i: (0, 0, 0))],
        out_specs=pl.BlockSpec((16, channels), lambda i: (0, 0)),
        compiler_params=params(16),
        cost_estimate=pl.CostEstimate(flops=1 << 16, bytes_accessed=1 << 17, transcendentals=0),
        name="edge",
    )(features)


def query_kernel(rows_ref, halo_ref, taps_ref, out_ref):
    value = rows_ref[0].astype(f32)
    lane = lax.broadcasted_iota(jnp.int32, value.shape, 1)
    halo = jnp.transpose(halo_ref[...].astype(f32))
    taps = taps_ref[:, 0, :]
    taps = jnp.transpose(jnp.concatenate([taps, jnp.zeros((5, taps.shape[1]), f32)], axis=0))
    once = jnp.where(lane == 0, halo[:, 15:16], pltpu.roll(value, 1, 1))
    twice = jnp.where(lane == 0, halo[:, 14:15], jnp.where(lane == 1, halo[:, 15:16], pltpu.roll(value, 2, 1)))
    out_ref[...] = taps[:, 0:1] * value + taps[:, 1:2] * once + taps[:, 2:3] * twice


def query_conv(features, halo, short_taps):
    channels, tokens = features.shape[1:]
    return pl.pallas_call(
        query_kernel,
        out_shape=jax.ShapeDtypeStruct((channels, tokens), f32),
        grid=(1,),
        in_specs=[
            pl.BlockSpec((1, channels, tokens), lambda i: (0, 0, 0)),
            pl.BlockSpec(halo.shape, lambda i: (0, 0)),
            pl.BlockSpec(short_taps.shape, lambda i: (0, 0, 0)),
        ],
        out_specs=pl.BlockSpec((channels, tokens), lambda i: (0, 0)),
        compiler_params=params(16),
        cost_estimate=pl.CostEstimate(flops=1 << 20, bytes_accessed=1 << 19, transcendentals=0),
        name="query_conv",
    )(features, halo, short_taps)


def gated_of(q_ref, mix_ref):
    return (q_ref[...] * mix_ref[...].astype(f32)).astype(bf16)


def give_kernel(member_ref, q_ref, mix_ref, weight_ref, out_ref):
    gated = gated_of(q_ref, mix_ref)
    width = mix_ref.shape[0]
    for chip in range(2):
        at = (2 * chip + 1 - member_ref[0] % 2) * width
        out_ref[chip * width : (chip + 1) * width, :] = jnp.dot(
            weight_ref[pl.ds(pl.multiple_of(at, width), width), :], gated, preferred_element_type=f32
        ).astype(bf16)


def keep_kernel(member_ref, q_ref, mix_ref, weight_ref, given_ref, out_ref):
    gated = gated_of(q_ref, mix_ref)
    width = mix_ref.shape[0]
    at = pl.multiple_of(member_ref[0] * width, width)
    chip = pl.multiple_of(member_ref[0] // 2 * width, width)
    own = jnp.dot(weight_ref[pl.ds(at, width), :], gated, preferred_element_type=f32)
    out_ref[...] = (own + given_ref[pl.ds(chip, width), :].astype(f32)).astype(out_ref.dtype)


def project(kernel, member, operands, rows, kind):
    in_vmem = pl.BlockSpec(memory_space=pltpu.VMEM)
    return pl.pallas_call(
        kernel,
        out_shape=jax.ShapeDtypeStruct((rows, operands[1].shape[1]), kind),
        in_specs=[pl.BlockSpec(memory_space=pltpu.SMEM)] + [in_vmem] * len(operands),
        out_specs=in_vmem,
        compiler_params=params(16),
        cost_estimate=pl.CostEstimate(flops=1 << 27, bytes_accessed=1 << 21, transcendentals=0),
    )(member, *operands)


def local(features, short_taps, filters, skip_gain, out_weight):
    chan_tp, tok_local = features.shape[1:]
    ctx_count = lax.axis_size("ctx")
    chan_dev = chan_tp // ctx_count
    rank = jnp.full((1,), lax.axis_index("ctx"), jnp.int32)
    member = jnp.full((1,), lax.axis_index("tp"), jnp.int32)

    sent = pack(in_hbm(features))
    got = lax.all_to_all(sent, "ctx", 0, 0, tiled=True)
    line, tiles = prepare(rank, *map(in_hbm, (filters, short_taps, skip_gain)))
    last = edge(in_hbm(features))
    halo = lax.ppermute(last, "ctx", [(i, i + 1) for i in range(ctx_count - 1)])
    mix = long_conv(got, line, tiles).reshape(ctx_count, chan_dev, tok_local)
    mix = lax.all_to_all(mix, "ctx", 0, 0, tiled=True).reshape(chan_tp, tok_local)
    q = query_conv(features, halo, short_taps)
    weight = turn(in_hbm(out_weight))
    given = project(give_kernel, member, (q, mix, weight), 2 * chan_tp, bf16)
    given = lax.ppermute(given, "tp", CORE_PAIRS)
    operands = (q, mix, weight, given)
    away = project(keep_kernel, lax.bitwise_xor(member, 2), operands, chan_tp, bf16)
    arrived = lax.ppermute(away, "tp", CHIP_PAIRS)
    home = project(keep_kernel, member, operands, chan_tp, f32)
    return (home + arrived.astype(f32)).astype(bf16)


def solution(mesh):
    placed = (P(None, "tp", "ctx"), P(None, None, "tp"), P("tp", None), P("tp"), P("tp", None))
    return jax.shard_map(
        local, mesh=mesh, in_specs=placed, out_specs=P("tp", "ctx"), check_vma=False
    )
```

```python
import jax
import jax.numpy as jnp
from jax import lax
from jax.experimental import pallas as pl
from jax.experimental.pallas import tpu as pltpu
from jax.sharding import PartitionSpec as P


GROUP = 16
LANES = 128
CHUNK = 1024
LEAD = 48
PACK_STEPS = 4
CORE_PAIRS = [(0, 1), (1, 0), (2, 3), (3, 2)]
CHIP_PAIRS = [(0, 2), (2, 0), (1, 3), (3, 1)]

f32 = jnp.float32
bf16 = jnp.bfloat16


def params(mib):
    return pltpu.CompilerParams(vmem_limit_bytes=mib << 20)


def in_hbm(array):
    return pltpu.with_memory_space_constraint(array, pltpu.HBM)


def fill_table(line_ref, table_ref, at):
    piece = line_ref[:, at : at + CHUNK + LANES]
    for tile in range(LANES // 16):
        moved = pltpu.roll(piece, 16 * tile, 1)[:, LANES:] if tile else piece[:, LANES:]
        for block in range(CHUNK // LANES):
            to_row = (block % 2) * LANES + 16 * tile
            to_col = (at // LANES + block) // 2 * LANES
            table_ref[to_row : to_row + 16, to_col : to_col + LANES] = moved[:, block * LANES : (block + 1) * LANES]


def pattern(values):
    row = lax.broadcasted_iota(jnp.int32, (8, LANES), 0) % len(values)
    tile = jnp.full((8, LANES), values[-1], f32)
    for index in range(len(values) - 1):
        tile = jnp.where(row == index, values[index], tile)
    return tile


def prepare_kernel(rank_ref, filters_ref, weight_ref, taps_ref, skip_ref, line_ref, tiles_ref, turned_ref, filter_ref, near_ref, wide_ref, sems):
    width = near_ref.shape[0]
    group = rank_ref[0] * 4 // GROUP
    first = rank_ref[0] * 4
    fetch = pltpu.make_async_copy(filters_ref.at[pl.ds(pl.multiple_of(group // 8 * 8, 8), 8)], filter_ref, sems.at[0])
    fetch.start()
    pieces = []
    for at in range(0, near_ref.shape[1], width):
        here = slice(at, at + width)
        pieces.append(pltpu.make_async_copy(weight_ref.at[:, here], near_ref.at[:, here], sems.at[1 + at // width]))
        pieces[-1].start()
    for offset in range(3):
        tiles_ref[offset] = pattern([taps_ref[offset, feature, first + c] for feature in (1, 2) for c in range(4)])
    tiles_ref[3] = pattern([skip_ref[first + c] for c in range(4)])
    wide_ref[:, : 2 * LANES] = jnp.zeros((8, 2 * LANES), f32)
    line_ref[:, :LANES] = jnp.zeros((16, LANES), bf16)
    fetch.wait()
    for at in range(0, filter_ref.shape[1], CHUNK):
        piece = filter_ref[:, at : at + CHUNK].astype(f32)
        sub = lax.broadcasted_iota(jnp.int32, piece.shape, 0)
        chosen = jnp.sum(jnp.where(sub == group % 8, piece, 0.0), axis=0, keepdims=True)
        wide_ref[:, 2 * LANES + at : 2 * LANES + at + CHUNK] = jnp.broadcast_to(chosen, piece.shape)
    for at in range(0, filter_ref.shape[1], CHUNK):
        piece = wide_ref[:, LANES + at : 2 * LANES + at + CHUNK]
        both = [pltpu.roll(piece, begin, 1, stride=1, stride_axis=0)[:, LANES:] for begin in (0, 8)]
        line_ref[:, LANES + at : LANES + at + CHUNK] = jnp.concatenate(both, axis=0).astype(bf16)
    for index, piece in enumerate(pieces):
        piece.wait()
        here = slice(index * width, (index + 1) * width)
        turned_ref[here, :] = jnp.transpose(near_ref[:, here])


def prepare(rank, filters, weight, short_taps, skip_gain):
    seq_len = filters.shape[1]
    in_smem = pl.BlockSpec(memory_space=pltpu.SMEM)
    in_place = pl.BlockSpec(memory_space=pltpu.HBM)
    in_vmem = pl.BlockSpec(memory_space=pltpu.VMEM)
    return pl.pallas_call(
        prepare_kernel,
        out_shape=[
            jax.ShapeDtypeStruct((16, LANES + seq_len), bf16),
            jax.ShapeDtypeStruct((4, 8, LANES), f32),
            jax.ShapeDtypeStruct(weight.shape[::-1], bf16),
        ],
        in_specs=[in_smem, in_place, in_place, in_smem, in_smem],
        out_specs=[in_vmem] * 3,
        scratch_shapes=[
            pltpu.VMEM((8, seq_len), bf16),
            pltpu.VMEM(weight.shape, bf16),
            pltpu.VMEM((8, 2 * LANES + seq_len), f32),
            pltpu.SemaphoreType.DMA((1 + weight.shape[1] // weight.shape[0],)),
        ],
        compiler_params=params(16),
        cost_estimate=pl.CostEstimate(flops=1 << 22, bytes_accessed=1 << 22, transcendentals=0),
        name="prepare",
    )(rank, filters, weight, short_taps, skip_gain)


def pack_kernel(features_ref, out_ref, rows_ref, packed_ref, in_sems, out_sems):
    rows = features_ref.shape[1] // PACK_STEPS
    fetches, stores = [], []
    for step in range(PACK_STEPS):
        here = slice(step * rows, (step + 1) * rows)
        fetches.append(pltpu.make_async_copy(features_ref.at[1:, here], rows_ref.at[:, here], in_sems.at[step]))
        fetches[-1].start()
    for step in range(PACK_STEPS):
        fetches[step].wait()
        k, v = (
            rows_ref[index, step * rows : (step + 1) * rows].astype(f32).reshape(rows // 8, 8, LANES) for index in range(2)
        )
        upper = lax.broadcasted_iota(jnp.int32, k.shape, 1) < 4
        even = jnp.where(upper, k, pltpu.roll(v, 4, 1))
        odd = jnp.where(upper, pltpu.roll(k, 4, 1), v)
        there = slice(step * rows // 4, (step + 1) * rows // 4)
        packed_ref[there] = jnp.stack([even, odd], axis=1).reshape(rows // 4, 8, LANES).astype(bf16)
        stores.append(pltpu.make_async_copy(packed_ref.at[there], out_ref.at[there], out_sems.at[step]))
        stores[-1].start()
    for store in stores:
        store.wait()


def pack(features):
    rows = features.shape[1]
    in_place = pl.BlockSpec(memory_space=pltpu.HBM)
    return pl.pallas_call(
        pack_kernel,
        out_shape=jax.ShapeDtypeStruct((rows // 4, 8, LANES), bf16),
        in_specs=[in_place],
        out_specs=in_place,
        scratch_shapes=[
            pltpu.VMEM((2, rows, LANES), bf16),
            pltpu.VMEM((rows // 4, 8, LANES), bf16),
            pltpu.SemaphoreType.DMA((PACK_STEPS,)),
            pltpu.SemaphoreType.DMA((PACK_STEPS,)),
        ],
        compiler_params=params(16),
        cost_estimate=pl.CostEstimate(flops=1 << 18, bytes_accessed=1 << 19, transcendentals=0),
        name="pack",
    )(features)


def conv_kernel(value_ref, line_ref, tiles_ref, out_ref, pair_ref, sum_ref, table_ref):
    blocks = value_ref.shape[0]
    rows = blocks * 4
    value = value_ref[...].astype(f32)
    lane = lax.broadcasted_iota(jnp.int32, value.shape, 2)
    sub = lax.broadcasted_iota(jnp.int32, (blocks // 2, 8, LANES), 1)

    def delayed(array):
        return jnp.concatenate([jnp.zeros((1, 8, LANES), f32), array[:-1]], axis=0)

    conv = tiles_ref[0][None] * value
    for offset in (1, 2):
        turned = pltpu.roll(value, offset, 2)
        conv = conv + tiles_ref[offset][None] * jnp.where(lane < offset, delayed(turned), turned)
    kv = (conv * pltpu.roll(conv, 4, 1)).astype(bf16).astype(f32)
    kv = kv.reshape(blocks // 2, 2, 8, LANES)
    even, odd = kv[:, 0], kv[:, 1]
    pair_ref[:LEAD, :] = jnp.zeros((LEAD, 2 * LANES), bf16)
    pair_ref[LEAD:, :LANES] = jnp.where(sub < 4, even, odd).reshape(rows, LANES).astype(bf16)
    pair_ref[LEAD:, LANES:] = jnp.where(sub < 4, delayed(odd), even).reshape(rows, LANES).astype(bf16)

    direct = tiles_ref[3][None]
    sum_ref[...] = (pair_ref[LEAD:, :LANES].astype(f32).reshape(rows // 8, 8, LANES) * direct).reshape(rows, LANES)
    for index in range(rows // 64):
        begin, base = 64 * index, CHUNK * index
        for at in (2 * base, 2 * base + CHUNK):
            fill_table(line_ref, table_ref, at)
        left = [pair_ref[LEAD - 16 * s : LEAD - 16 * s + rows - begin, :] for s in range(4)]
        right = [table_ref[:, base + 256 * s : base + 256 * (s + 1)] for s in range(4)]
        moved = jnp.dot(
            jnp.concatenate(left, axis=1), jnp.concatenate(right, axis=0), preferred_element_type=f32
        )
        sum_ref[begin:, :] += moved[:, :LANES]
        sum_ref[begin + 8 :, :] += moved[: rows - begin - 8, LANES:]
    out_ref[...] = sum_ref[...].astype(bf16)


def long_conv(value, line, tiles):
    rows = value.shape[0] * 4
    seq_len = line.shape[1] - LANES
    in_vmem = pl.BlockSpec(memory_space=pltpu.VMEM)
    return pl.pallas_call(
        conv_kernel,
        out_shape=jax.ShapeDtypeStruct((rows, LANES), bf16),
        in_specs=[in_vmem] * 3,
        out_specs=in_vmem,
        scratch_shapes=[
            pltpu.VMEM((LEAD + rows, 2 * LANES), bf16),
            pltpu.VMEM((rows, LANES), f32),
            pltpu.VMEM((2 * LANES, seq_len // 2), bf16),
        ],
        compiler_params=params(16),
        cost_estimate=pl.CostEstimate(flops=1 << 31, bytes_accessed=1 << 20, transcendentals=0),
        name="long_conv",
    )(value, line, tiles)


def edge_kernel(rows_ref, out_ref):
    out_ref[...] = jnp.transpose(rows_ref[0])[LANES - 16 :, :]


def edge(features):
    channels, tokens = features.shape[1:]
    return pl.pallas_call(
        edge_kernel,
        out_shape=jax.ShapeDtypeStruct((16, channels), bf16),
        grid=(1,),
        in_specs=[pl.BlockSpec((1, channels, tokens), lambda i: (0, 0, 0))],
        out_specs=pl.BlockSpec((16, channels), lambda i: (0, 0)),
        compiler_params=params(16),
        cost_estimate=pl.CostEstimate(flops=1 << 16, bytes_accessed=1 << 17, transcendentals=0),
        name="edge",
    )(features)


def query_kernel(rows_ref, halo_ref, taps_ref, out_ref):
    value = rows_ref[0].astype(f32)
    lane = lax.broadcasted_iota(jnp.int32, value.shape, 1)
    halo = jnp.transpose(halo_ref[...].astype(f32))
    taps = taps_ref[:, 0, :]
    taps = jnp.transpose(jnp.concatenate([taps, jnp.zeros((5, taps.shape[1]), f32)], axis=0))
    once = jnp.where(lane == 0, halo[:, 15:16], pltpu.roll(value, 1, 1))
    twice = jnp.where(lane == 0, halo[:, 14:15], jnp.where(lane == 1, halo[:, 15:16], pltpu.roll(value, 2, 1)))
    out_ref[...] = taps[:, 0:1] * value + taps[:, 1:2] * once + taps[:, 2:3] * twice


def query_conv(features, halo, short_taps):
    channels, tokens = features.shape[1:]
    return pl.pallas_call(
        query_kernel,
        out_shape=jax.ShapeDtypeStruct((channels, tokens), f32),
        grid=(1,),
        in_specs=[
            pl.BlockSpec((1, channels, tokens), lambda i: (0, 0, 0)),
            pl.BlockSpec(halo.shape, lambda i: (0, 0)),
            pl.BlockSpec(short_taps.shape, lambda i: (0, 0, 0)),
        ],
        out_specs=pl.BlockSpec((channels, tokens), lambda i: (0, 0)),
        compiler_params=params(16),
        cost_estimate=pl.CostEstimate(flops=1 << 20, bytes_accessed=1 << 19, transcendentals=0),
        name="query_conv",
    )(features, halo, short_taps)


def gated_of(q_ref, mix_ref):
    return (q_ref[...] * mix_ref[...].astype(f32)).astype(bf16)


def give_kernel(member_ref, q_ref, mix_ref, weight_ref, out_ref):
    gated = gated_of(q_ref, mix_ref)
    width = mix_ref.shape[0]
    for chip in range(2):
        at = (2 * chip + 1 - member_ref[0] % 2) * width
        out_ref[chip * width : (chip + 1) * width, :] = jnp.dot(
            weight_ref[pl.ds(pl.multiple_of(at, width), width), :], gated, preferred_element_type=f32
        ).astype(bf16)


def keep_kernel(member_ref, q_ref, mix_ref, weight_ref, given_ref, out_ref):
    gated = gated_of(q_ref, mix_ref)
    width = mix_ref.shape[0]
    at = pl.multiple_of(member_ref[0] * width, width)
    chip = pl.multiple_of(member_ref[0] // 2 * width, width)
    own = jnp.dot(weight_ref[pl.ds(at, width), :], gated, preferred_element_type=f32)
    out_ref[...] = (own + given_ref[pl.ds(chip, width), :].astype(f32)).astype(out_ref.dtype)


def project(kernel, member, operands, rows, kind):
    in_vmem = pl.BlockSpec(memory_space=pltpu.VMEM)
    return pl.pallas_call(
        kernel,
        out_shape=jax.ShapeDtypeStruct((rows, operands[1].shape[1]), kind),
        in_specs=[pl.BlockSpec(memory_space=pltpu.SMEM)] + [in_vmem] * len(operands),
        out_specs=in_vmem,
        compiler_params=params(16),
        cost_estimate=pl.CostEstimate(flops=1 << 27, bytes_accessed=1 << 21, transcendentals=0),
    )(member, *operands)


def local(features, short_taps, filters, skip_gain, out_weight):
    chan_tp, tok_local = features.shape[1:]
    ctx_count = lax.axis_size("ctx")
    chan_dev = chan_tp // ctx_count
    rank = jnp.full((1,), lax.axis_index("ctx"), jnp.int32)
    member = jnp.full((1,), lax.axis_index("tp"), jnp.int32)

    sent = pack(in_hbm(features))
    got = lax.all_to_all(sent, "ctx", 0, 0, tiled=True)
    last = edge(in_hbm(features))
    halo = lax.ppermute(last, "ctx", [(i, i + 1) for i in range(ctx_count - 1)])
    line, tiles, weight = prepare(rank, *map(in_hbm, (filters, out_weight, short_taps, skip_gain)))
    q = query_conv(in_hbm(features), halo, short_taps)

    mix = long_conv(got, line, tiles).reshape(ctx_count, chan_dev, tok_local)
    mix, member = lax.optimization_barrier((mix, member))
    mix = lax.all_to_all(mix, "ctx", 0, 0, tiled=True).reshape(chan_tp, tok_local)
    given = project(give_kernel, member, (q, mix, weight), 2 * chan_tp, bf16)
    given = lax.ppermute(given, "tp", CORE_PAIRS)
    operands = (q, mix, weight, given)
    away = project(keep_kernel, lax.bitwise_xor(member, 2), operands, chan_tp, bf16)
    arrived = lax.ppermute(away, "tp", CHIP_PAIRS)
    home = project(keep_kernel, member, operands, chan_tp, f32)
    return (home + arrived.astype(f32)).astype(bf16)


def solution(mesh):
    placed = (P(None, "tp", "ctx"), P(None, None, "tp"), P("tp", None), P("tp"), P("tp", None))
    return jax.shard_map(
        local, mesh=mesh, in_specs=placed, out_specs=P("tp", "ctx"), check_vma=False
    )
```

```python
import jax
import jax.numpy as jnp
from jax import lax
from jax.experimental import pallas as pl
from jax.experimental.pallas import tpu as pltpu
from jax.sharding import PartitionSpec as P


GROUP = 16
LANES = 128
CHUNK = 1024
LEAD = 48
PACK_STEPS = 4
OUT_STEPS = 4
CORE_PAIRS = [(0, 1), (1, 0), (2, 3), (3, 2)]
CHIP_PAIRS = [(0, 2), (2, 0), (1, 3), (3, 1)]

f32 = jnp.float32
bf16 = jnp.bfloat16


def params(mib):
    return pltpu.CompilerParams(vmem_limit_bytes=mib << 20)


def in_hbm(array):
    return pltpu.with_memory_space_constraint(array, pltpu.HBM)


def fill_table(line_ref, table_ref, at):
    piece = line_ref[:, at : at + CHUNK + LANES]
    for tile in range(LANES // 16):
        moved = pltpu.roll(piece, 16 * tile, 1)[:, LANES:] if tile else piece[:, LANES:]
        for block in range(CHUNK // LANES):
            to_row = (block % 2) * LANES + 16 * tile
            to_col = (at // LANES + block) // 2 * LANES
            table_ref[to_row : to_row + 16, to_col : to_col + LANES] = moved[:, block * LANES : (block + 1) * LANES]


def pattern(values):
    row = lax.broadcasted_iota(jnp.int32, (8, LANES), 0) % len(values)
    tile = jnp.full((8, LANES), values[-1], f32)
    for index in range(len(values) - 1):
        tile = jnp.where(row == index, values[index], tile)
    return tile


def prepare_kernel(rank_ref, filter_ref, taps_ref, skip_ref, line_ref, tiles_ref, wide_ref):
    own = (rank_ref[0] * 4 // GROUP) % 8
    first = rank_ref[0] * 4
    wide_ref[:, : 2 * LANES] = jnp.zeros((8, 2 * LANES), f32)
    line_ref[:, :LANES] = jnp.zeros((16, LANES), bf16)
    for at in range(0, filter_ref.shape[1], CHUNK):
        piece = filter_ref[:, at : at + CHUNK].astype(f32)
        sub = lax.broadcasted_iota(jnp.int32, piece.shape, 0)
        chosen = jnp.sum(jnp.where(sub == own, piece, 0.0), axis=0, keepdims=True)
        wide_ref[:, 2 * LANES + at : 2 * LANES + at + CHUNK] = jnp.broadcast_to(chosen, piece.shape)
    for at in range(0, filter_ref.shape[1], CHUNK):
        piece = wide_ref[:, LANES + at : 2 * LANES + at + CHUNK]
        both = [pltpu.roll(piece, begin, 1, stride=1, stride_axis=0)[:, LANES:] for begin in (0, 8)]
        line_ref[:, LANES + at : LANES + at + CHUNK] = jnp.concatenate(both, axis=0).astype(bf16)
    for offset in range(3):
        tiles_ref[offset] = pattern([taps_ref[offset, feature, first + c] for feature in (1, 2) for c in range(4)])
    tiles_ref[3] = pattern([skip_ref[first + c] for c in range(4)])


def prepare(rank, filters, short_taps, skip_gain):
    seq_len = filters.shape[1]
    in_smem = pl.BlockSpec(memory_space=pltpu.SMEM)
    return pl.pallas_call(
        prepare_kernel,
        out_shape=[
            jax.ShapeDtypeStruct((16, LANES + seq_len), bf16),
            jax.ShapeDtypeStruct((4, 8, LANES), f32),
        ],
        grid_spec=pltpu.PrefetchScalarGridSpec(
            num_scalar_prefetch=1,
            grid=(1,),
            in_specs=[pl.BlockSpec((8, seq_len), lambda i, r: (r[0] * 4 // GROUP // 8, 0)), in_smem, in_smem],
            out_specs=[
                pl.BlockSpec((16, LANES + seq_len), lambda i, r: (0, 0)),
                pl.BlockSpec((4, 8, LANES), lambda i, r: (0, 0, 0)),
            ],
            scratch_shapes=[pltpu.VMEM((8, 2 * LANES + seq_len), f32)],
        ),
        compiler_params=params(16),
        cost_estimate=pl.CostEstimate(flops=1 << 22, bytes_accessed=1 << 20, transcendentals=0),
        name="prepare",
    )(rank, filters, short_taps, skip_gain)


def pack_kernel(features_ref, out_ref, rows_ref, packed_ref, in_sems, out_sems):
    rows = features_ref.shape[1] // PACK_STEPS
    fetches, stores = [], []
    for step in range(PACK_STEPS):
        here = slice(step * rows, (step + 1) * rows)
        fetches.append(pltpu.make_async_copy(features_ref.at[1:, here], rows_ref.at[:, here], in_sems.at[step]))
        fetches[-1].start()
    for step in range(PACK_STEPS):
        fetches[step].wait()
        k, v = (
            rows_ref[index, step * rows : (step + 1) * rows].astype(f32).reshape(rows // 8, 8, LANES) for index in range(2)
        )
        upper = lax.broadcasted_iota(jnp.int32, k.shape, 1) < 4
        even = jnp.where(upper, k, pltpu.roll(v, 4, 1))
        odd = jnp.where(upper, pltpu.roll(k, 4, 1), v)
        there = slice(step * rows // 4, (step + 1) * rows // 4)
        packed_ref[there] = jnp.stack([even, odd], axis=1).reshape(rows // 4, 8, LANES).astype(bf16)
        stores.append(pltpu.make_async_copy(packed_ref.at[there], out_ref.at[there], out_sems.at[step]))
        stores[-1].start()
    for store in stores:
        store.wait()


def pack(features):
    rows = features.shape[1]
    in_place = pl.BlockSpec(memory_space=pltpu.HBM)
    return pl.pallas_call(
        pack_kernel,
        out_shape=jax.ShapeDtypeStruct((rows // 4, 8, LANES), bf16),
        in_specs=[in_place],
        out_specs=in_place,
        scratch_shapes=[
            pltpu.VMEM((2, rows, LANES), bf16),
            pltpu.VMEM((rows // 4, 8, LANES), bf16),
            pltpu.SemaphoreType.DMA((PACK_STEPS,)),
            pltpu.SemaphoreType.DMA((PACK_STEPS,)),
        ],
        compiler_params=params(16),
        cost_estimate=pl.CostEstimate(flops=1 << 18, bytes_accessed=1 << 19, transcendentals=0),
        name="pack",
    )(features)


def conv_kernel(value_ref, line_ref, tiles_ref, out_ref, pair_ref, sum_ref, table_ref, mix_ref, sems):
    blocks = value_ref.shape[0]
    rows = blocks * 4
    value = value_ref[...].astype(f32)
    lane = lax.broadcasted_iota(jnp.int32, value.shape, 2)
    sub = lax.broadcasted_iota(jnp.int32, (blocks // 2, 8, LANES), 1)

    def delayed(array):
        return jnp.concatenate([jnp.zeros((1, 8, LANES), f32), array[:-1]], axis=0)

    conv = tiles_ref[0][None] * value
    for offset in (1, 2):
        turned = pltpu.roll(value, offset, 2)
        conv = conv + tiles_ref[offset][None] * jnp.where(lane < offset, delayed(turned), turned)
    kv = (conv * pltpu.roll(conv, 4, 1)).astype(bf16).astype(f32)
    kv = kv.reshape(blocks // 2, 2, 8, LANES)
    even, odd = kv[:, 0], kv[:, 1]
    pair_ref[:LEAD, :] = jnp.zeros((LEAD, 2 * LANES), bf16)
    pair_ref[LEAD:, :LANES] = jnp.where(sub < 4, even, odd).reshape(rows, LANES).astype(bf16)
    pair_ref[LEAD:, LANES:] = jnp.where(sub < 4, delayed(odd), even).reshape(rows, LANES).astype(bf16)

    direct = tiles_ref[3][None]
    sum_ref[...] = (pair_ref[LEAD:, :LANES].astype(f32).reshape(rows // 8, 8, LANES) * direct).reshape(rows, LANES)
    for index in range(rows // 64):
        for at in (2 * CHUNK * index, 2 * CHUNK * index + CHUNK):
            fill_table(line_ref, table_ref, at)
        if index:
            add_shifted(pair_ref, table_ref, sum_ref, index, 0, rows - 64 * index)
    stretch = rows // OUT_STEPS
    leaving = []
    for begin in range(0, rows, stretch):
        add_shifted(pair_ref, table_ref, sum_ref, 0, begin, min(stretch, rows - begin))
        here = slice(begin, begin + stretch)
        mix_ref[here, :] = sum_ref[here, :].astype(bf16)
        leaving.append(pltpu.make_async_copy(mix_ref.at[here], out_ref.at[here], sems.at[begin // stretch]))
        leaving[-1].start()
    for copy in leaving:
        copy.wait()


def add_shifted(pair_ref, table_ref, sum_ref, index, first, count):
    base = CHUNK * index
    left = [pair_ref[LEAD + first - 16 * s : LEAD + first - 16 * s + count, :] for s in range(4)]
    right = [table_ref[:, base + 256 * s : base + 256 * (s + 1)] for s in range(4)]
    moved = jnp.dot(jnp.concatenate(left, axis=1), jnp.concatenate(right, axis=0), preferred_element_type=f32)
    begin = 64 * index + first
    rows = sum_ref.shape[0]
    sum_ref[begin : begin + count, :] += moved[:, :LANES]
    count = min(count, rows - begin - 8)
    sum_ref[begin + 8 : begin + 8 + count, :] += moved[:count, LANES:]


def long_conv(value, line, tiles):
    rows = value.shape[0] * 4
    seq_len = line.shape[1] - LANES
    in_vmem = pl.BlockSpec(memory_space=pltpu.VMEM)
    return pl.pallas_call(
        conv_kernel,
        out_shape=jax.ShapeDtypeStruct((rows, LANES), bf16),
        in_specs=[in_vmem] * 3,
        out_specs=pl.BlockSpec(memory_space=pltpu.HBM),
        scratch_shapes=[
            pltpu.VMEM((LEAD + rows, 2 * LANES), bf16),
            pltpu.VMEM((rows, LANES), f32),
            pltpu.VMEM((2 * LANES, seq_len // 2), bf16),
            pltpu.VMEM((rows, LANES), bf16),
            pltpu.SemaphoreType.DMA((OUT_STEPS,)),
        ],
        compiler_params=params(16),
        cost_estimate=pl.CostEstimate(flops=1 << 31, bytes_accessed=1 << 20, transcendentals=0),
        name="long_conv",
    )(value, line, tiles)


def turn_kernel(weight_ref, out_ref):
    out_ref[...] = jnp.transpose(weight_ref[...])


def turn(weight):
    width, total = weight.shape
    return pl.pallas_call(
        turn_kernel,
        out_shape=jax.ShapeDtypeStruct((total, width), bf16),
        grid=(total // width,),
        in_specs=[pl.BlockSpec((width, width), lambda i: (0, i))],
        out_specs=pl.BlockSpec((width, width), lambda i: (i, 0)),
        compiler_params=params(16),
        cost_estimate=pl.CostEstimate(flops=1 << 20, bytes_accessed=1 << 22, transcendentals=0),
        name="turn",
    )(weight)


def edge_kernel(rows_ref, out_ref):
    out_ref[...] = jnp.transpose(rows_ref[0])[LANES - 16 :, :]


def edge(features):
    channels, tokens = features.shape[1:]
    return pl.pallas_call(
        edge_kernel,
        out_shape=jax.ShapeDtypeStruct((16, channels), bf16),
        grid=(1,),
        in_specs=[pl.BlockSpec((1, channels, tokens), lambda i: (0, 0, 0))],
        out_specs=pl.BlockSpec((16, channels), lambda i: (0, 0)),
        compiler_params=params(16),
        cost_estimate=pl.CostEstimate(flops=1 << 16, bytes_accessed=1 << 17, transcendentals=0),
        name="edge",
    )(features)


def query_kernel(rows_ref, halo_ref, taps_ref, out_ref):
    value = rows_ref[0].astype(f32)
    lane = lax.broadcasted_iota(jnp.int32, value.shape, 1)
    halo = jnp.transpose(halo_ref[...].astype(f32))
    taps = taps_ref[:, 0, :]
    taps = jnp.transpose(jnp.concatenate([taps, jnp.zeros((5, taps.shape[1]), f32)], axis=0))
    once = jnp.where(lane == 0, halo[:, 15:16], pltpu.roll(value, 1, 1))
    twice = jnp.where(lane == 0, halo[:, 14:15], jnp.where(lane == 1, halo[:, 15:16], pltpu.roll(value, 2, 1)))
    out_ref[...] = taps[:, 0:1] * value + taps[:, 1:2] * once + taps[:, 2:3] * twice


def query_conv(features, halo, short_taps):
    channels, tokens = features.shape[1:]
    return pl.pallas_call(
        query_kernel,
        out_shape=jax.ShapeDtypeStruct((channels, tokens), f32),
        grid=(1,),
        in_specs=[
            pl.BlockSpec((1, channels, tokens), lambda i: (0, 0, 0)),
            pl.BlockSpec(halo.shape, lambda i: (0, 0)),
            pl.BlockSpec(short_taps.shape, lambda i: (0, 0, 0)),
        ],
        out_specs=pl.BlockSpec((channels, tokens), lambda i: (0, 0)),
        compiler_params=params(16),
        cost_estimate=pl.CostEstimate(flops=1 << 20, bytes_accessed=1 << 19, transcendentals=0),
        name="query_conv",
    )(features, halo, short_taps)


def gated_of(q_ref, mix_ref):
    return (q_ref[...] * mix_ref[...].astype(f32)).astype(bf16)


def own_part(member, q_ref, mix_ref, weight_ref):
    width = mix_ref.shape[0]
    at = pl.multiple_of(member * width, width)
    return jnp.dot(weight_ref[pl.ds(at, width), :], gated_of(q_ref, mix_ref), preferred_element_type=f32)


def give_kernel(member_ref, q_ref, mix_ref, weight_ref, out_ref):
    out_ref[...] = own_part(member_ref[0], q_ref, mix_ref, weight_ref).astype(bf16)


def keep_kernel(member_ref, q_ref, mix_ref, weight_ref, given_ref, out_ref):
    own = own_part(member_ref[0], q_ref, mix_ref, weight_ref)
    out_ref[...] = (own + given_ref[...].astype(f32)).astype(out_ref.dtype)


def project(kernel, member, operands, rows, kind):
    in_vmem = pl.BlockSpec(memory_space=pltpu.VMEM)
    return pl.pallas_call(
        kernel,
        out_shape=jax.ShapeDtypeStruct((rows, operands[1].shape[1]), kind),
        in_specs=[pl.BlockSpec(memory_space=pltpu.SMEM)] + [in_vmem] * len(operands),
        out_specs=in_vmem,
        compiler_params=params(16),
        cost_estimate=pl.CostEstimate(flops=1 << 27, bytes_accessed=1 << 21, transcendentals=0),
    )(member, *operands)


def local(features, short_taps, filters, skip_gain, out_weight):
    chan_tp, tok_local = features.shape[1:]
    ctx_count = lax.axis_size("ctx")
    chan_dev = chan_tp // ctx_count
    rank = jnp.full((1,), lax.axis_index("ctx"), jnp.int32)
    member = jnp.full((1,), lax.axis_index("tp"), jnp.int32)

    sent = pack(in_hbm(features))
    got = lax.all_to_all(sent, "ctx", 0, 0, tiled=True)
    line, tiles = prepare(rank, *map(in_hbm, (filters, short_taps, skip_gain)))
    last = edge(in_hbm(features))
    halo = lax.ppermute(last, "ctx", [(i, i + 1) for i in range(ctx_count - 1)])
    mix = long_conv(got, line, tiles).reshape(ctx_count, chan_dev, tok_local)
    mix = lax.all_to_all(mix, "ctx", 0, 0, tiled=True).reshape(chan_tp, tok_local)
    q = query_conv(features, halo, short_taps)
    weight = turn(in_hbm(out_weight))
    operands = (q, mix, weight)
    rows = chan_tp
    given = project(give_kernel, lax.bitwise_xor(member, 3), operands, rows, bf16)
    given = lax.ppermute(given, "tp", CORE_PAIRS)
    away = project(keep_kernel, lax.bitwise_xor(member, 2), (*operands, given), rows, bf16)
    arrived = lax.ppermute(away, "tp", CHIP_PAIRS)
    given_home = project(give_kernel, lax.bitwise_xor(member, 1), operands, rows, bf16)
    given_home = lax.ppermute(given_home, "tp", CORE_PAIRS)
    home = project(keep_kernel, member, (*operands, given_home), rows, f32)
    return (home + arrived.astype(f32)).astype(bf16)


def solution(mesh):
    placed = (P(None, "tp", "ctx"), P(None, None, "tp"), P("tp", None), P("tp"), P("tp", None))
    return jax.shard_map(
        local, mesh=mesh, in_specs=placed, out_specs=P("tp", "ctx"), check_vma=False
    )
```

```python
import jax
import jax.numpy as jnp
from jax import lax
from jax.experimental import pallas as pl
from jax.experimental.pallas import tpu as pltpu
from jax.sharding import PartitionSpec as P


GROUP = 16
LANES = 128
CHUNK = 1024
LEAD = 48
PACK_STEPS = 4
CORE_PAIRS = [(0, 1), (1, 0), (2, 3), (3, 2)]
CHIP_PAIRS = [(0, 2), (2, 0), (1, 3), (3, 1)]

f32 = jnp.float32
bf16 = jnp.bfloat16


def params(mib):
    return pltpu.CompilerParams(vmem_limit_bytes=mib << 20)


def in_hbm(array):
    return pltpu.with_memory_space_constraint(array, pltpu.HBM)


def fill_table(line_ref, table_ref, at):
    piece = line_ref[:, at : at + CHUNK + LANES]
    for tile in range(LANES // 16):
        moved = pltpu.roll(piece, 16 * tile, 1)[:, LANES:] if tile else piece[:, LANES:]
        for block in range(CHUNK // LANES):
            to_row = (block % 2) * LANES + 16 * tile
            to_col = (at // LANES + block) // 2 * LANES
            table_ref[to_row : to_row + 16, to_col : to_col + LANES] = moved[:, block * LANES : (block + 1) * LANES]


def pattern(values):
    row = lax.broadcasted_iota(jnp.int32, (8, LANES), 0) % len(values)
    tile = jnp.full((8, LANES), values[-1], f32)
    for index in range(len(values) - 1):
        tile = jnp.where(row == index, values[index], tile)
    return tile


def prepare_kernel(rank_ref, filter_ref, taps_ref, skip_ref, line_ref, tiles_ref, wide_ref):
    own = (rank_ref[0] * 4 // GROUP) % 8
    first = rank_ref[0] * 4
    wide_ref[:, : 2 * LANES] = jnp.zeros((8, 2 * LANES), f32)
    line_ref[:, :LANES] = jnp.zeros((16, LANES), bf16)
    for at in range(0, filter_ref.shape[1], CHUNK):
        piece = filter_ref[:, at : at + CHUNK].astype(f32)
        sub = lax.broadcasted_iota(jnp.int32, piece.shape, 0)
        chosen = jnp.sum(jnp.where(sub == own, piece, 0.0), axis=0, keepdims=True)
        wide_ref[:, 2 * LANES + at : 2 * LANES + at + CHUNK] = jnp.broadcast_to(chosen, piece.shape)
    for at in range(0, filter_ref.shape[1], CHUNK):
        piece = wide_ref[:, LANES + at : 2 * LANES + at + CHUNK]
        both = [pltpu.roll(piece, begin, 1, stride=1, stride_axis=0)[:, LANES:] for begin in (0, 8)]
        line_ref[:, LANES + at : LANES + at + CHUNK] = jnp.concatenate(both, axis=0).astype(bf16)
    for offset in range(3):
        tiles_ref[offset] = pattern([taps_ref[offset, feature, first + c] for feature in (1, 2) for c in range(4)])
    tiles_ref[3] = pattern([skip_ref[first + c] for c in range(4)])


def prepare(rank, filters, short_taps, skip_gain):
    seq_len = filters.shape[1]
    in_smem = pl.BlockSpec(memory_space=pltpu.SMEM)
    return pl.pallas_call(
        prepare_kernel,
        out_shape=[
            jax.ShapeDtypeStruct((16, LANES + seq_len), bf16),
            jax.ShapeDtypeStruct((4, 8, LANES), f32),
        ],
        grid_spec=pltpu.PrefetchScalarGridSpec(
            num_scalar_prefetch=1,
            grid=(1,),
            in_specs=[pl.BlockSpec((8, seq_len), lambda i, r: (r[0] * 4 // GROUP // 8, 0)), in_smem, in_smem],
            out_specs=[
                pl.BlockSpec((16, LANES + seq_len), lambda i, r: (0, 0)),
                pl.BlockSpec((4, 8, LANES), lambda i, r: (0, 0, 0)),
            ],
            scratch_shapes=[pltpu.VMEM((8, 2 * LANES + seq_len), f32)],
        ),
        compiler_params=params(16),
        cost_estimate=pl.CostEstimate(flops=1 << 22, bytes_accessed=1 << 20, transcendentals=0),
        name="prepare",
    )(rank, filters, short_taps, skip_gain)


def pack_kernel(features_ref, out_ref, sems):
    blocks = out_ref.shape[0] // PACK_STEPS
    copies = []
    for row in range(2):
        for step in range(PACK_STEPS):
            here = slice(step * blocks, (step + 1) * blocks)
            copies.append(
                pltpu.make_async_copy(
                    features_ref.at[1 + row, here], out_ref.at[here, row], sems.at[row * PACK_STEPS + step]
                )
            )
            copies[-1].start()
    for copy in copies:
        copy.wait()


def pack(features):
    rows, blocks, channels, tokens = features.shape
    in_place = pl.BlockSpec(memory_space=pltpu.HBM)
    return pl.pallas_call(
        pack_kernel,
        out_shape=jax.ShapeDtypeStruct((blocks, rows - 1, channels, tokens), bf16),
        in_specs=[in_place],
        out_specs=in_place,
        scratch_shapes=[pltpu.SemaphoreType.DMA((2 * PACK_STEPS,))],
        compiler_params=params(16),
        cost_estimate=pl.CostEstimate(flops=1 << 18, bytes_accessed=1 << 19, transcendentals=0),
        name="pack",
    )(in_hbm(features))


def conv_kernel(value_ref, line_ref, tiles_ref, out_ref, pair_ref, sum_ref, table_ref):
    blocks = value_ref.shape[0]
    rows = blocks * 4
    value = value_ref[...].astype(f32)
    lane = lax.broadcasted_iota(jnp.int32, value.shape, 2)
    sub = lax.broadcasted_iota(jnp.int32, (blocks // 2, 8, LANES), 1)

    def delayed(array):
        return jnp.concatenate([jnp.zeros((1, 8, LANES), f32), array[:-1]], axis=0)

    conv = tiles_ref[0][None] * value
    for offset in (1, 2):
        turned = pltpu.roll(value, offset, 2)
        conv = conv + tiles_ref[offset][None] * jnp.where(lane < offset, delayed(turned), turned)
    kv = (conv * pltpu.roll(conv, 4, 1)).astype(bf16).astype(f32)
    kv = kv.reshape(blocks // 2, 2, 8, LANES)
    even, odd = kv[:, 0], kv[:, 1]
    pair_ref[:LEAD, :] = jnp.zeros((LEAD, 2 * LANES), bf16)
    pair_ref[LEAD:, :LANES] = jnp.where(sub < 4, even, odd).reshape(rows, LANES).astype(bf16)
    pair_ref[LEAD:, LANES:] = jnp.where(sub < 4, delayed(odd), even).reshape(rows, LANES).astype(bf16)

    direct = tiles_ref[3][None]
    sum_ref[...] = (pair_ref[LEAD:, :LANES].astype(f32).reshape(rows // 8, 8, LANES) * direct).reshape(rows, LANES)
    for index in range(rows // 64):
        begin, base = 64 * index, CHUNK * index
        for at in (2 * base, 2 * base + CHUNK):
            fill_table(line_ref, table_ref, at)
        left = [pair_ref[LEAD - 16 * s : LEAD - 16 * s + rows - begin, :] for s in range(4)]
        right = [table_ref[:, base + 256 * s : base + 256 * (s + 1)] for s in range(4)]
        moved = jnp.dot(
            jnp.concatenate(left, axis=1), jnp.concatenate(right, axis=0), preferred_element_type=f32
        )
        sum_ref[begin:, :] += moved[:, :LANES]
        sum_ref[begin + 8 :, :] += moved[: rows - begin - 8, LANES:]
    out_ref[...] = sum_ref[...].astype(bf16)


def long_conv(value, line, tiles):
    rows = value.shape[0] * 4
    seq_len = line.shape[1] - LANES
    in_vmem = pl.BlockSpec(memory_space=pltpu.VMEM)
    return pl.pallas_call(
        conv_kernel,
        out_shape=jax.ShapeDtypeStruct((rows, LANES), bf16),
        in_specs=[in_vmem] * 3,
        out_specs=in_vmem,
        scratch_shapes=[
            pltpu.VMEM((LEAD + rows, 2 * LANES), bf16),
            pltpu.VMEM((rows, LANES), f32),
            pltpu.VMEM((2 * LANES, seq_len // 2), bf16),
        ],
        compiler_params=params(16),
        cost_estimate=pl.CostEstimate(flops=1 << 31, bytes_accessed=1 << 20, transcendentals=0),
        name="long_conv",
    )(value, line, tiles)


def turn_kernel(weight_ref, out_ref):
    out_ref[...] = jnp.transpose(weight_ref[...])


def turn(weight):
    width, total = weight.shape
    return pl.pallas_call(
        turn_kernel,
        out_shape=jax.ShapeDtypeStruct((total, width), bf16),
        grid=(total // width,),
        in_specs=[pl.BlockSpec((width, width), lambda i: (0, i))],
        out_specs=pl.BlockSpec((width, width), lambda i: (i, 0)),
        compiler_params=params(16),
        cost_estimate=pl.CostEstimate(flops=1 << 20, bytes_accessed=1 << 22, transcendentals=0),
        name="turn",
    )(weight)


def edge_kernel(rows_ref, out_ref):
    out_ref[...] = jnp.transpose(rows_ref[0])[LANES - 16 :, :]


def edge(features):
    channels, tokens = features.shape[1:]
    return pl.pallas_call(
        edge_kernel,
        out_shape=jax.ShapeDtypeStruct((16, channels), bf16),
        grid=(1,),
        in_specs=[pl.BlockSpec((1, channels, tokens), lambda i: (0, 0, 0))],
        out_specs=pl.BlockSpec((16, channels), lambda i: (0, 0)),
        compiler_params=params(16),
        cost_estimate=pl.CostEstimate(flops=1 << 16, bytes_accessed=1 << 17, transcendentals=0),
        name="edge",
    )(features)


def query_kernel(rows_ref, halo_ref, taps_ref, out_ref):
    value = rows_ref[0].astype(f32)
    lane = lax.broadcasted_iota(jnp.int32, value.shape, 1)
    halo = jnp.transpose(halo_ref[...].astype(f32))
    taps = taps_ref[:, 0, :]
    taps = jnp.transpose(jnp.concatenate([taps, jnp.zeros((5, taps.shape[1]), f32)], axis=0))
    once = jnp.where(lane == 0, halo[:, 15:16], pltpu.roll(value, 1, 1))
    twice = jnp.where(lane == 0, halo[:, 14:15], jnp.where(lane == 1, halo[:, 15:16], pltpu.roll(value, 2, 1)))
    out_ref[...] = taps[:, 0:1] * value + taps[:, 1:2] * once + taps[:, 2:3] * twice


def query_conv(features, halo, short_taps):
    channels, tokens = features.shape[1:]
    return pl.pallas_call(
        query_kernel,
        out_shape=jax.ShapeDtypeStruct((channels, tokens), f32),
        grid=(1,),
        in_specs=[
            pl.BlockSpec((1, channels, tokens), lambda i: (0, 0, 0)),
            pl.BlockSpec(halo.shape, lambda i: (0, 0)),
            pl.BlockSpec(short_taps.shape, lambda i: (0, 0, 0)),
        ],
        out_specs=pl.BlockSpec((channels, tokens), lambda i: (0, 0)),
        compiler_params=params(16),
        cost_estimate=pl.CostEstimate(flops=1 << 20, bytes_accessed=1 << 19, transcendentals=0),
        name="query_conv",
    )(features, halo, short_taps)


def gated_of(q_ref, mix_ref):
    return (q_ref[...] * mix_ref[...].astype(f32)).astype(bf16)


def own_part(member, q_ref, mix_ref, weight_ref):
    width = mix_ref.shape[0]
    at = pl.multiple_of(member * width, width)
    return jnp.dot(weight_ref[pl.ds(at, width), :], gated_of(q_ref, mix_ref), preferred_element_type=f32)


def give_kernel(member_ref, q_ref, mix_ref, weight_ref, out_ref):
    out_ref[...] = own_part(member_ref[0], q_ref, mix_ref, weight_ref).astype(bf16)


def keep_kernel(member_ref, q_ref, mix_ref, weight_ref, given_ref, out_ref):
    own = own_part(member_ref[0], q_ref, mix_ref, weight_ref)
    out_ref[...] = (own + given_ref[...].astype(f32)).astype(out_ref.dtype)


def project(kernel, member, operands, rows, kind):
    in_vmem = pl.BlockSpec(memory_space=pltpu.VMEM)
    return pl.pallas_call(
        kernel,
        out_shape=jax.ShapeDtypeStruct((rows, operands[1].shape[1]), kind),
        in_specs=[pl.BlockSpec(memory_space=pltpu.SMEM)] + [in_vmem] * len(operands),
        out_specs=in_vmem,
        compiler_params=params(16),
        cost_estimate=pl.CostEstimate(flops=1 << 27, bytes_accessed=1 << 21, transcendentals=0),
    )(member, *operands)


def local(features, short_taps, filters, skip_gain, out_weight):
    chan_tp, tok_local = features.shape[1:]
    ctx_count = lax.axis_size("ctx")
    chan_dev = chan_tp // ctx_count
    rank = jnp.full((1,), lax.axis_index("ctx"), jnp.int32)
    member = jnp.full((1,), lax.axis_index("tp"), jnp.int32)

    sent = pack(features.reshape(features.shape[0], ctx_count, chan_dev, tok_local))
    got = lax.all_to_all(sent, "ctx", 0, 0, tiled=True).reshape(ctx_count, 2 * chan_dev, tok_local)
    line, tiles = prepare(rank, *map(in_hbm, (filters, short_taps, skip_gain)))
    last = edge(in_hbm(features))
    halo = lax.ppermute(last, "ctx", [(i, i + 1) for i in range(ctx_count - 1)])
    mix = long_conv(got, line, tiles).reshape(ctx_count, chan_dev, tok_local)
    mix = lax.all_to_all(mix, "ctx", 0, 0, tiled=True).reshape(chan_tp, tok_local)
    q = query_conv(features, halo, short_taps)
    weight = turn(in_hbm(out_weight))
    operands = (q, mix, weight)
    rows = chan_tp
    given = project(give_kernel, lax.bitwise_xor(member, 3), operands, rows, bf16)
    given = lax.ppermute(given, "tp", CORE_PAIRS)
    away = project(keep_kernel, lax.bitwise_xor(member, 2), (*operands, given), rows, bf16)
    arrived = lax.ppermute(away, "tp", CHIP_PAIRS)
    given_home = project(give_kernel, lax.bitwise_xor(member, 1), operands, rows, bf16)
    given_home = lax.ppermute(given_home, "tp", CORE_PAIRS)
    home = project(keep_kernel, member, (*operands, given_home), rows, f32)
    return (home + arrived.astype(f32)).astype(bf16)


def solution(mesh):
    placed = (P(None, "tp", "ctx"), P(None, None, "tp"), P("tp", None), P("tp"), P("tp", None))
    return jax.shard_map(
        local, mesh=mesh, in_specs=placed, out_specs=P("tp", "ctx"), check_vma=False
    )
```

```python
import jax
import jax.numpy as jnp
from jax import lax
from jax.experimental import pallas as pl
from jax.experimental.pallas import tpu as pltpu
from jax.sharding import PartitionSpec as P


GROUP = 16
LANES = 128
CHUNK = 1024
LEAD = 48
PACK_STEPS = 4
CORE_PAIRS = [(0, 1), (1, 0), (2, 3), (3, 2)]
CHIP_PAIRS = [(0, 2), (2, 0), (1, 3), (3, 1)]

f32 = jnp.float32
bf16 = jnp.bfloat16


def params(mib):
    return pltpu.CompilerParams(vmem_limit_bytes=mib << 20)


def in_hbm(array):
    return pltpu.with_memory_space_constraint(array, pltpu.HBM)


def fill_table(line_ref, table_ref, at):
    piece = line_ref[:, at : at + CHUNK + LANES]
    for tile in range(LANES // 16):
        moved = pltpu.roll(piece, 16 * tile, 1)[:, LANES:] if tile else piece[:, LANES:]
        for block in range(CHUNK // LANES):
            to_row = (block % 2) * LANES + 16 * tile
            to_col = (at // LANES + block) // 2 * LANES
            table_ref[to_row : to_row + 16, to_col : to_col + LANES] = moved[:, block * LANES : (block + 1) * LANES]


def pattern(values):
    row = lax.broadcasted_iota(jnp.int32, (8, LANES), 0) % len(values)
    tile = jnp.full((8, LANES), values[-1], f32)
    for index in range(len(values) - 1):
        tile = jnp.where(row == index, values[index], tile)
    return tile


def prepare_kernel(rank_ref, filter_ref, taps_ref, skip_ref, line_ref, tiles_ref, wide_ref):
    own = (rank_ref[0] * 4 // GROUP) % 8
    first = rank_ref[0] * 4
    wide_ref[:, : 2 * LANES] = jnp.zeros((8, 2 * LANES), f32)
    line_ref[:, :LANES] = jnp.zeros((16, LANES), bf16)
    for at in range(0, filter_ref.shape[1], CHUNK):
        piece = filter_ref[:, at : at + CHUNK].astype(f32)
        sub = lax.broadcasted_iota(jnp.int32, piece.shape, 0)
        chosen = jnp.sum(jnp.where(sub == own, piece, 0.0), axis=0, keepdims=True)
        wide_ref[:, 2 * LANES + at : 2 * LANES + at + CHUNK] = jnp.broadcast_to(chosen, piece.shape)
    for at in range(0, filter_ref.shape[1], CHUNK):
        piece = wide_ref[:, LANES + at : 2 * LANES + at + CHUNK]
        both = [pltpu.roll(piece, begin, 1, stride=1, stride_axis=0)[:, LANES:] for begin in (0, 8)]
        line_ref[:, LANES + at : LANES + at + CHUNK] = jnp.concatenate(both, axis=0).astype(bf16)
    for offset in range(3):
        tiles_ref[offset] = pattern([taps_ref[offset, feature, first + c] for feature in (1, 2) for c in range(4)])
    tiles_ref[3] = pattern([skip_ref[first + c] for c in range(4)])


def prepare(rank, filters, short_taps, skip_gain):
    seq_len = filters.shape[1]
    in_smem = pl.BlockSpec(memory_space=pltpu.SMEM)
    return pl.pallas_call(
        prepare_kernel,
        out_shape=[
            jax.ShapeDtypeStruct((16, LANES + seq_len), bf16),
            jax.ShapeDtypeStruct((4, 8, LANES), f32),
        ],
        grid_spec=pltpu.PrefetchScalarGridSpec(
            num_scalar_prefetch=1,
            grid=(1,),
            in_specs=[pl.BlockSpec((8, seq_len), lambda i, r: (r[0] * 4 // GROUP // 8, 0)), in_smem, in_smem],
            out_specs=[
                pl.BlockSpec((16, LANES + seq_len), lambda i, r: (0, 0)),
                pl.BlockSpec((4, 8, LANES), lambda i, r: (0, 0, 0)),
            ],
            scratch_shapes=[pltpu.VMEM((8, 2 * LANES + seq_len), f32)],
        ),
        compiler_params=params(16),
        cost_estimate=pl.CostEstimate(flops=1 << 22, bytes_accessed=1 << 20, transcendentals=0),
        name="prepare",
    )(rank, filters, short_taps, skip_gain)


def pack_kernel(features_ref, out_ref, rows_ref, packed_ref, in_sems, out_sems):
    rows = features_ref.shape[1] // PACK_STEPS
    fetches, stores = [], []
    for step in range(PACK_STEPS):
        here = slice(step * rows, (step + 1) * rows)
        fetches.append(pltpu.make_async_copy(features_ref.at[1:, here], rows_ref.at[:, here], in_sems.at[step]))
        fetches[-1].start()
    for step in range(PACK_STEPS):
        fetches[step].wait()
        k, v = (
            rows_ref[index, step * rows : (step + 1) * rows].astype(f32).reshape(rows // 8, 8, LANES) for index in range(2)
        )
        upper = lax.broadcasted_iota(jnp.int32, k.shape, 1) < 4
        even = jnp.where(upper, k, pltpu.roll(v, 4, 1))
        odd = jnp.where(upper, pltpu.roll(k, 4, 1), v)
        there = slice(step * rows // 4, (step + 1) * rows // 4)
        packed_ref[there] = jnp.stack([even, odd], axis=1).reshape(rows // 4, 8, LANES).astype(bf16)
        stores.append(pltpu.make_async_copy(packed_ref.at[there], out_ref.at[there], out_sems.at[step]))
        stores[-1].start()
    for store in stores:
        store.wait()


def pack(features):
    rows = features.shape[1]
    in_place = pl.BlockSpec(memory_space=pltpu.HBM)
    return pl.pallas_call(
        pack_kernel,
        out_shape=jax.ShapeDtypeStruct((rows // 4, 8, LANES), bf16),
        in_specs=[in_place],
        out_specs=in_place,
        scratch_shapes=[
            pltpu.VMEM((2, rows, LANES), bf16),
            pltpu.VMEM((rows // 4, 8, LANES), bf16),
            pltpu.SemaphoreType.DMA((PACK_STEPS,)),
            pltpu.SemaphoreType.DMA((PACK_STEPS,)),
        ],
        compiler_params=params(16),
        cost_estimate=pl.CostEstimate(flops=1 << 18, bytes_accessed=1 << 19, transcendentals=0),
        name="pack",
    )(features)


def conv_kernel(value_ref, line_ref, tiles_ref, out_ref, pair_ref, sum_ref, table_ref):
    blocks = value_ref.shape[0]
    rows = blocks * 4
    value = value_ref[...].astype(f32)
    lane = lax.broadcasted_iota(jnp.int32, value.shape, 2)
    sub = lax.broadcasted_iota(jnp.int32, (blocks // 2, 8, LANES), 1)

    def delayed(array):
        return jnp.concatenate([jnp.zeros((1, 8, LANES), f32), array[:-1]], axis=0)

    conv = tiles_ref[0][None] * value
    for offset in (1, 2):
        turned = pltpu.roll(value, offset, 2)
        conv = conv + tiles_ref[offset][None] * jnp.where(lane < offset, delayed(turned), turned)
    kv = (conv * pltpu.roll(conv, 4, 1)).astype(bf16).astype(f32)
    kv = kv.reshape(blocks // 2, 2, 8, LANES)
    even, odd = kv[:, 0], kv[:, 1]
    pair_ref[:LEAD, :] = jnp.zeros((LEAD, 2 * LANES), bf16)
    pair_ref[LEAD:, :LANES] = jnp.where(sub < 4, even, odd).reshape(rows, LANES).astype(bf16)
    pair_ref[LEAD:, LANES:] = jnp.where(sub < 4, delayed(odd), even).reshape(rows, LANES).astype(bf16)

    direct = tiles_ref[3][None]
    sum_ref[...] = (pair_ref[LEAD:, :LANES].astype(f32).reshape(rows // 8, 8, LANES) * direct).reshape(rows, LANES)
    for index in range(rows // 64):
        begin, base = 64 * index, CHUNK * index
        for at in (2 * base, 2 * base + CHUNK):
            fill_table(line_ref, table_ref, at)
        left = [pair_ref[LEAD - 16 * s : LEAD - 16 * s + rows - begin, :] for s in range(4)]
        right = [table_ref[:, base + 256 * s : base + 256 * (s + 1)] for s in range(4)]
        moved = jnp.dot(
            jnp.concatenate(left, axis=1), jnp.concatenate(right, axis=0), preferred_element_type=f32
        )
        sum_ref[begin:, :] += moved[:, :LANES]
        sum_ref[begin + 8 :, :] += moved[: rows - begin - 8, LANES:]
    out_ref[...] = sum_ref[...].astype(bf16)


def long_conv(value, line, tiles):
    rows = value.shape[0] * 4
    seq_len = line.shape[1] - LANES
    in_vmem = pl.BlockSpec(memory_space=pltpu.VMEM)
    return pl.pallas_call(
        conv_kernel,
        out_shape=jax.ShapeDtypeStruct((rows, LANES), bf16),
        in_specs=[in_vmem] * 3,
        out_specs=in_vmem,
        scratch_shapes=[
            pltpu.VMEM((LEAD + rows, 2 * LANES), bf16),
            pltpu.VMEM((rows, LANES), f32),
            pltpu.VMEM((2 * LANES, seq_len // 2), bf16),
        ],
        compiler_params=params(16),
        cost_estimate=pl.CostEstimate(flops=1 << 31, bytes_accessed=1 << 20, transcendentals=0),
        name="long_conv",
    )(value, line, tiles)


def turn_kernel(weight_ref, out_ref):
    out_ref[...] = jnp.transpose(weight_ref[...])


def turn(weight):
    width, total = weight.shape
    return pl.pallas_call(
        turn_kernel,
        out_shape=jax.ShapeDtypeStruct((total, width), bf16),
        grid=(total // width,),
        in_specs=[pl.BlockSpec((width, width), lambda i: (0, i))],
        out_specs=pl.BlockSpec((width, width), lambda i: (i, 0)),
        compiler_params=params(16),
        cost_estimate=pl.CostEstimate(flops=1 << 20, bytes_accessed=1 << 22, transcendentals=0),
        name="turn",
    )(weight)


def edge_kernel(rows_ref, out_ref):
    out_ref[...] = jnp.transpose(rows_ref[0])[LANES - 16 :, :]


def edge(features):
    channels, tokens = features.shape[1:]
    return pl.pallas_call(
        edge_kernel,
        out_shape=jax.ShapeDtypeStruct((16, channels), bf16),
        grid=(1,),
        in_specs=[pl.BlockSpec((1, channels, tokens), lambda i: (0, 0, 0))],
        out_specs=pl.BlockSpec((16, channels), lambda i: (0, 0)),
        compiler_params=params(16),
        cost_estimate=pl.CostEstimate(flops=1 << 16, bytes_accessed=1 << 17, transcendentals=0),
        name="edge",
    )(features)


def query_kernel(rows_ref, halo_ref, taps_ref, out_ref):
    value = rows_ref[0].astype(f32)
    lane = lax.broadcasted_iota(jnp.int32, value.shape, 1)
    halo = jnp.transpose(halo_ref[...].astype(f32))
    taps = taps_ref[:, 0, :]
    taps = jnp.transpose(jnp.concatenate([taps, jnp.zeros((5, taps.shape[1]), f32)], axis=0))
    once = jnp.where(lane == 0, halo[:, 15:16], pltpu.roll(value, 1, 1))
    twice = jnp.where(lane == 0, halo[:, 14:15], jnp.where(lane == 1, halo[:, 15:16], pltpu.roll(value, 2, 1)))
    out_ref[...] = taps[:, 0:1] * value + taps[:, 1:2] * once + taps[:, 2:3] * twice


def query_conv(features, halo, short_taps):
    channels, tokens = features.shape[1:]
    return pl.pallas_call(
        query_kernel,
        out_shape=jax.ShapeDtypeStruct((channels, tokens), f32),
        grid=(1,),
        in_specs=[
            pl.BlockSpec((1, channels, tokens), lambda i: (0, 0, 0)),
            pl.BlockSpec(halo.shape, lambda i: (0, 0)),
            pl.BlockSpec(short_taps.shape, lambda i: (0, 0, 0)),
        ],
        out_specs=pl.BlockSpec((channels, tokens), lambda i: (0, 0)),
        compiler_params=params(16),
        cost_estimate=pl.CostEstimate(flops=1 << 20, bytes_accessed=1 << 19, transcendentals=0),
        name="query_conv",
    )(features, halo, short_taps)


def gated_of(q_ref, mix_ref):
    return (q_ref[...] * mix_ref[...].astype(f32)).astype(bf16)


def own_part(member, q_ref, mix_ref, weight_ref):
    width = mix_ref.shape[0]
    at = pl.multiple_of(member * width, width)
    return jnp.dot(weight_ref[pl.ds(at, width), :], gated_of(q_ref, mix_ref), preferred_element_type=f32)


def give_kernel(member_ref, q_ref, mix_ref, weight_ref, out_ref):
    out_ref[...] = own_part(member_ref[0], q_ref, mix_ref, weight_ref).astype(bf16)


def keep_kernel(member_ref, q_ref, mix_ref, weight_ref, given_ref, out_ref):
    own = own_part(member_ref[0], q_ref, mix_ref, weight_ref)
    out_ref[...] = (own + given_ref[...].astype(f32)).astype(out_ref.dtype)


def project(kernel, member, operands, rows, kind):
    in_vmem = pl.BlockSpec(memory_space=pltpu.VMEM)
    return pl.pallas_call(
        kernel,
        out_shape=jax.ShapeDtypeStruct((rows, operands[1].shape[1]), kind),
        in_specs=[pl.BlockSpec(memory_space=pltpu.SMEM)] + [in_vmem] * len(operands),
        out_specs=in_vmem,
        compiler_params=params(16),
        cost_estimate=pl.CostEstimate(flops=1 << 27, bytes_accessed=1 << 21, transcendentals=0),
    )(member, *operands)


def local(features, short_taps, filters, skip_gain, out_weight):
    chan_tp, tok_local = features.shape[1:]
    ctx_count = lax.axis_size("ctx")
    chan_dev = chan_tp // ctx_count
    rank = jnp.full((1,), lax.axis_index("ctx"), jnp.int32)
    member = jnp.full((1,), lax.axis_index("tp"), jnp.int32)

    sent = pack(in_hbm(features))
    got = lax.all_to_all(sent, "ctx", 0, 0, tiled=True)
    line, tiles = prepare(rank, *map(in_hbm, (filters, short_taps, skip_gain)))
    last = edge(in_hbm(features))
    halo = lax.ppermute(last, "ctx", [(i, i + 1) for i in range(ctx_count - 1)])
    mix = long_conv(got, line, tiles).reshape(ctx_count, chan_dev, tok_local)
    mix = lax.all_to_all(mix, "ctx", 0, 0, tiled=True).reshape(chan_tp, tok_local)
    q = query_conv(features, halo, short_taps)
    weight = turn(in_hbm(out_weight))
    operands = (q, mix, weight)
    rows = chan_tp
    given = project(give_kernel, lax.bitwise_xor(member, 3), operands, rows, bf16)
    given = lax.ppermute(given, "tp", CORE_PAIRS)
    away = project(keep_kernel, lax.bitwise_xor(member, 2), (*operands, given), rows, bf16)
    arrived = lax.ppermute(away, "tp", CHIP_PAIRS)
    given_home = project(give_kernel, lax.bitwise_xor(member, 1), operands, rows, bf16)
    given_home = lax.ppermute(given_home, "tp", CORE_PAIRS)
    home = project(keep_kernel, member, (*operands, given_home), rows, f32)
    return (home + arrived.astype(f32)).astype(bf16)


def solution(mesh):
    placed = (P(None, "tp", "ctx"), P(None, None, "tp"), P("tp", None), P("tp"), P("tp", None))
    return jax.shard_map(
        local, mesh=mesh, in_specs=placed, out_specs=P("tp", "ctx"), check_vma=False
    )
```

```python
import jax
import jax.numpy as jnp
from jax import lax
from jax.experimental import pallas as pl
from jax.experimental.pallas import tpu as pltpu
from jax.sharding import PartitionSpec as P


GROUP = 16
LANES = 128
CHUNK = 1024
LEAD = 48
PACK_STEPS = 4
CORE_PAIRS = [(0, 1), (1, 0), (2, 3), (3, 2)]
CHIP_PAIRS = [(0, 2), (2, 0), (1, 3), (3, 1)]

f32 = jnp.float32
bf16 = jnp.bfloat16


def params(mib):
    return pltpu.CompilerParams(vmem_limit_bytes=mib << 20)


def in_hbm(array):
    return pltpu.with_memory_space_constraint(array, pltpu.HBM)


def fill_table(line_ref, table_ref, at):
    piece = line_ref[:, at : at + CHUNK + LANES]
    for tile in range(LANES // 16):
        moved = pltpu.roll(piece, 16 * tile, 1)[:, LANES:] if tile else piece[:, LANES:]
        for block in range(CHUNK // LANES):
            to_row = (block % 2) * LANES + 16 * tile
            to_col = (at // LANES + block) // 2 * LANES
            table_ref[to_row : to_row + 16, to_col : to_col + LANES] = moved[:, block * LANES : (block + 1) * LANES]


def pattern(values):
    row = lax.broadcasted_iota(jnp.int32, (8, LANES), 0) % len(values)
    tile = jnp.full((8, LANES), values[-1], f32)
    for index in range(len(values) - 1):
        tile = jnp.where(row == index, values[index], tile)
    return tile


def prepare_kernel(rank_ref, filter_ref, taps_ref, skip_ref, line_ref, tiles_ref, wide_ref):
    own = (rank_ref[0] * 4 // GROUP) % 8
    first = rank_ref[0] * 4
    wide_ref[:, : 2 * LANES] = jnp.zeros((8, 2 * LANES), f32)
    line_ref[:, :LANES] = jnp.zeros((16, LANES), bf16)
    for at in range(0, filter_ref.shape[1], CHUNK):
        piece = filter_ref[:, at : at + CHUNK].astype(f32)
        sub = lax.broadcasted_iota(jnp.int32, piece.shape, 0)
        chosen = jnp.sum(jnp.where(sub == own, piece, 0.0), axis=0, keepdims=True)
        wide_ref[:, 2 * LANES + at : 2 * LANES + at + CHUNK] = jnp.broadcast_to(chosen, piece.shape)
    for at in range(0, filter_ref.shape[1], CHUNK):
        piece = wide_ref[:, LANES + at : 2 * LANES + at + CHUNK]
        both = [pltpu.roll(piece, begin, 1, stride=1, stride_axis=0)[:, LANES:] for begin in (0, 8)]
        line_ref[:, LANES + at : LANES + at + CHUNK] = jnp.concatenate(both, axis=0).astype(bf16)
    for offset in range(3):
        tiles_ref[offset] = pattern([taps_ref[offset, feature, first + c] for feature in (1, 2) for c in range(4)])
    tiles_ref[3] = pattern([skip_ref[first + c] for c in range(4)])


def prepare(rank, filters, short_taps, skip_gain):
    seq_len = filters.shape[1]
    in_smem = pl.BlockSpec(memory_space=pltpu.SMEM)
    return pl.pallas_call(
        prepare_kernel,
        out_shape=[
            jax.ShapeDtypeStruct((16, LANES + seq_len), bf16),
            jax.ShapeDtypeStruct((4, 8, LANES), f32),
        ],
        grid_spec=pltpu.PrefetchScalarGridSpec(
            num_scalar_prefetch=1,
            grid=(1,),
            in_specs=[pl.BlockSpec((8, seq_len), lambda i, r: (r[0] * 4 // GROUP // 8, 0)), in_smem, in_smem],
            out_specs=[
                pl.BlockSpec((16, LANES + seq_len), lambda i, r: (0, 0)),
                pl.BlockSpec((4, 8, LANES), lambda i, r: (0, 0, 0)),
            ],
            scratch_shapes=[pltpu.VMEM((8, 2 * LANES + seq_len), f32)],
        ),
        compiler_params=params(16),
        cost_estimate=pl.CostEstimate(flops=1 << 22, bytes_accessed=1 << 20, transcendentals=0),
        name="prepare",
    )(rank, filters, short_taps, skip_gain)


def pack_kernel(features_ref, out_ref, rows_ref, packed_ref, in_sems, out_sems):
    rows = features_ref.shape[1] // PACK_STEPS
    fetches, stores = [], []
    for step in range(PACK_STEPS):
        here = slice(step * rows, (step + 1) * rows)
        fetches.append(pltpu.make_async_copy(features_ref.at[1:, here], rows_ref.at[:, here], in_sems.at[step]))
        fetches[-1].start()
    for step in range(PACK_STEPS):
        fetches[step].wait()
        k, v = (
            rows_ref[index, step * rows : (step + 1) * rows].astype(f32).reshape(rows // 8, 8, LANES) for index in range(2)
        )
        upper = lax.broadcasted_iota(jnp.int32, k.shape, 1) < 4
        even = jnp.where(upper, k, pltpu.roll(v, 4, 1))
        odd = jnp.where(upper, pltpu.roll(k, 4, 1), v)
        after = (step + PACK_STEPS // 2) % PACK_STEPS
        there = slice(after * rows // 4, (after + 1) * rows // 4)
        packed_ref[there] = jnp.stack([even, odd], axis=1).reshape(rows // 4, 8, LANES).astype(bf16)
        stores.append(pltpu.make_async_copy(packed_ref.at[there], out_ref.at[there], out_sems.at[step]))
        stores[-1].start()
    for store in stores:
        store.wait()


def pack(features):
    rows = features.shape[1]
    in_place = pl.BlockSpec(memory_space=pltpu.HBM)
    return pl.pallas_call(
        pack_kernel,
        out_shape=jax.ShapeDtypeStruct((rows // 4, 8, LANES), bf16),
        in_specs=[in_place],
        out_specs=in_place,
        scratch_shapes=[
            pltpu.VMEM((2, rows, LANES), bf16),
            pltpu.VMEM((rows // 4, 8, LANES), bf16),
            pltpu.SemaphoreType.DMA((PACK_STEPS,)),
            pltpu.SemaphoreType.DMA((PACK_STEPS,)),
        ],
        compiler_params=params(16),
        cost_estimate=pl.CostEstimate(flops=1 << 18, bytes_accessed=1 << 19, transcendentals=0),
        name="pack",
    )(features)


def conv_kernel(value_ref, line_ref, tiles_ref, out_ref, pair_ref, sum_ref, table_ref):
    blocks = value_ref.shape[0]
    rows = blocks * 4
    value = jnp.concatenate([value_ref[blocks // 2 :], value_ref[: blocks // 2]], axis=0).astype(f32)
    lane = lax.broadcasted_iota(jnp.int32, value.shape, 2)
    sub = lax.broadcasted_iota(jnp.int32, (blocks // 2, 8, LANES), 1)

    def delayed(array):
        return jnp.concatenate([jnp.zeros((1, 8, LANES), f32), array[:-1]], axis=0)

    conv = tiles_ref[0][None] * value
    for offset in (1, 2):
        turned = pltpu.roll(value, offset, 2)
        conv = conv + tiles_ref[offset][None] * jnp.where(lane < offset, delayed(turned), turned)
    kv = (conv * pltpu.roll(conv, 4, 1)).astype(bf16).astype(f32)
    kv = kv.reshape(blocks // 2, 2, 8, LANES)
    even, odd = kv[:, 0], kv[:, 1]
    pair_ref[:LEAD, :] = jnp.zeros((LEAD, 2 * LANES), bf16)
    pair_ref[LEAD:, :LANES] = jnp.where(sub < 4, even, odd).reshape(rows, LANES).astype(bf16)
    pair_ref[LEAD:, LANES:] = jnp.where(sub < 4, delayed(odd), even).reshape(rows, LANES).astype(bf16)

    direct = tiles_ref[3][None]
    sum_ref[...] = (pair_ref[LEAD:, :LANES].astype(f32).reshape(rows // 8, 8, LANES) * direct).reshape(rows, LANES)
    for index in range(rows // 64):
        begin, base = 64 * index, CHUNK * index
        for at in (2 * base, 2 * base + CHUNK):
            fill_table(line_ref, table_ref, at)
        left = [pair_ref[LEAD - 16 * s : LEAD - 16 * s + rows - begin, :] for s in range(4)]
        right = [table_ref[:, base + 256 * s : base + 256 * (s + 1)] for s in range(4)]
        moved = jnp.dot(
            jnp.concatenate(left, axis=1), jnp.concatenate(right, axis=0), preferred_element_type=f32
        )
        sum_ref[begin:, :] += moved[:, :LANES]
        sum_ref[begin + 8 :, :] += moved[: rows - begin - 8, LANES:]
    out_ref[...] = sum_ref[...].astype(bf16)


def long_conv(value, line, tiles):
    rows = value.shape[0] * 4
    seq_len = line.shape[1] - LANES
    in_vmem = pl.BlockSpec(memory_space=pltpu.VMEM)
    return pl.pallas_call(
        conv_kernel,
        out_shape=jax.ShapeDtypeStruct((rows, LANES), bf16),
        in_specs=[in_vmem] * 3,
        out_specs=in_vmem,
        scratch_shapes=[
            pltpu.VMEM((LEAD + rows, 2 * LANES), bf16),
            pltpu.VMEM((rows, LANES), f32),
            pltpu.VMEM((2 * LANES, seq_len // 2), bf16),
        ],
        compiler_params=params(16),
        cost_estimate=pl.CostEstimate(flops=1 << 31, bytes_accessed=1 << 20, transcendentals=0),
        name="long_conv",
    )(value, line, tiles)


def turn_kernel(weight_ref, out_ref):
    out_ref[...] = jnp.transpose(weight_ref[...])


def turn(weight):
    width, total = weight.shape
    return pl.pallas_call(
        turn_kernel,
        out_shape=jax.ShapeDtypeStruct((total, width), bf16),
        grid=(total // width,),
        in_specs=[pl.BlockSpec((width, width), lambda i: (0, i))],
        out_specs=pl.BlockSpec((width, width), lambda i: (i, 0)),
        compiler_params=params(16),
        cost_estimate=pl.CostEstimate(flops=1 << 20, bytes_accessed=1 << 22, transcendentals=0),
        name="turn",
    )(weight)


def edge_kernel(rows_ref, out_ref):
    out_ref[...] = jnp.transpose(rows_ref[0])[LANES - 16 :, :]


def edge(features):
    channels, tokens = features.shape[1:]
    return pl.pallas_call(
        edge_kernel,
        out_shape=jax.ShapeDtypeStruct((16, channels), bf16),
        grid=(1,),
        in_specs=[pl.BlockSpec((1, channels, tokens), lambda i: (0, 0, 0))],
        out_specs=pl.BlockSpec((16, channels), lambda i: (0, 0)),
        compiler_params=params(16),
        cost_estimate=pl.CostEstimate(flops=1 << 16, bytes_accessed=1 << 17, transcendentals=0),
        name="edge",
    )(features)


def query_kernel(rows_ref, halo_ref, taps_ref, out_ref):
    value = rows_ref[0].astype(f32)
    lane = lax.broadcasted_iota(jnp.int32, value.shape, 1)
    halo = jnp.transpose(halo_ref[...].astype(f32))
    taps = taps_ref[:, 0, :]
    taps = jnp.transpose(jnp.concatenate([taps, jnp.zeros((5, taps.shape[1]), f32)], axis=0))
    once = jnp.where(lane == 0, halo[:, 15:16], pltpu.roll(value, 1, 1))
    twice = jnp.where(lane == 0, halo[:, 14:15], jnp.where(lane == 1, halo[:, 15:16], pltpu.roll(value, 2, 1)))
    out_ref[...] = taps[:, 0:1] * value + taps[:, 1:2] * once + taps[:, 2:3] * twice


def query_conv(features, halo, short_taps):
    channels, tokens = features.shape[1:]
    return pl.pallas_call(
        query_kernel,
        out_shape=jax.ShapeDtypeStruct((channels, tokens), f32),
        grid=(1,),
        in_specs=[
            pl.BlockSpec((1, channels, tokens), lambda i: (0, 0, 0)),
            pl.BlockSpec(halo.shape, lambda i: (0, 0)),
            pl.BlockSpec(short_taps.shape, lambda i: (0, 0, 0)),
        ],
        out_specs=pl.BlockSpec((channels, tokens), lambda i: (0, 0)),
        compiler_params=params(16),
        cost_estimate=pl.CostEstimate(flops=1 << 20, bytes_accessed=1 << 19, transcendentals=0),
        name="query_conv",
    )(features, halo, short_taps)


def gated_of(q_ref, mix_ref):
    return (q_ref[...] * mix_ref[...].astype(f32)).astype(bf16)


def own_part(member, q_ref, mix_ref, weight_ref):
    width = mix_ref.shape[0]
    at = pl.multiple_of(member * width, width)
    return jnp.dot(weight_ref[pl.ds(at, width), :], gated_of(q_ref, mix_ref), preferred_element_type=f32)


def give_kernel(member_ref, q_ref, mix_ref, weight_ref, out_ref):
    out_ref[...] = own_part(member_ref[0], q_ref, mix_ref, weight_ref).astype(bf16)


def keep_kernel(member_ref, q_ref, mix_ref, weight_ref, given_ref, out_ref):
    own = own_part(member_ref[0], q_ref, mix_ref, weight_ref)
    out_ref[...] = (own + given_ref[...].astype(f32)).astype(out_ref.dtype)


def project(kernel, member, operands, rows, kind):
    in_vmem = pl.BlockSpec(memory_space=pltpu.VMEM)
    return pl.pallas_call(
        kernel,
        out_shape=jax.ShapeDtypeStruct((rows, operands[1].shape[1]), kind),
        in_specs=[pl.BlockSpec(memory_space=pltpu.SMEM)] + [in_vmem] * len(operands),
        out_specs=in_vmem,
        compiler_params=params(16),
        cost_estimate=pl.CostEstimate(flops=1 << 27, bytes_accessed=1 << 21, transcendentals=0),
    )(member, *operands)


def local(features, short_taps, filters, skip_gain, out_weight):
    chan_tp, tok_local = features.shape[1:]
    ctx_count = lax.axis_size("ctx")
    chan_dev = chan_tp // ctx_count
    rank = jnp.full((1,), lax.axis_index("ctx"), jnp.int32)
    member = jnp.full((1,), lax.axis_index("tp"), jnp.int32)

    sent = pack(in_hbm(features))
    order = [(i + ctx_count // 2) % ctx_count for i in range(ctx_count)]
    got = lax.all_to_all(sent, "ctx", 0, 0, axis_index_groups=[order], tiled=True)
    line, tiles = prepare(rank, *map(in_hbm, (filters, short_taps, skip_gain)))
    last = edge(in_hbm(features))
    halo = lax.ppermute(last, "ctx", [(i, i + 1) for i in range(ctx_count - 1)])
    mix = long_conv(got, line, tiles).reshape(ctx_count, chan_dev, tok_local)
    mix = lax.all_to_all(mix, "ctx", 0, 0, tiled=True).reshape(chan_tp, tok_local)
    q = query_conv(features, halo, short_taps)
    weight = turn(in_hbm(out_weight))
    operands = (q, mix, weight)
    rows = chan_tp
    given = project(give_kernel, lax.bitwise_xor(member, 3), operands, rows, bf16)
    given = lax.ppermute(given, "tp", CORE_PAIRS)
    away = project(keep_kernel, lax.bitwise_xor(member, 2), (*operands, given), rows, bf16)
    arrived = lax.ppermute(away, "tp", CHIP_PAIRS)
    given_home = project(give_kernel, lax.bitwise_xor(member, 1), operands, rows, bf16)
    given_home = lax.ppermute(given_home, "tp", CORE_PAIRS)
    home = project(keep_kernel, member, (*operands, given_home), rows, f32)
    return (home + arrived.astype(f32)).astype(bf16)


def solution(mesh):
    placed = (P(None, "tp", "ctx"), P(None, None, "tp"), P("tp", None), P("tp"), P("tp", None))
    return jax.shard_map(
        local, mesh=mesh, in_specs=placed, out_specs=P("tp", "ctx"), check_vma=False
    )
```

```python
import jax
import jax.numpy as jnp
from jax import lax
from jax.experimental import pallas as pl
from jax.experimental.pallas import tpu as pltpu
from jax.sharding import PartitionSpec as P


GROUP = 16
LANES = 128
CHUNK = 1024
LEAD = 48
PACK_STEPS = 4
CORE_PAIRS = [(0, 1), (1, 0), (2, 3), (3, 2)]
CHIP_PAIRS = [(0, 2), (2, 0), (1, 3), (3, 1)]

f32 = jnp.float32
bf16 = jnp.bfloat16


def params(mib):
    return pltpu.CompilerParams(vmem_limit_bytes=mib << 20)


def in_hbm(array):
    return pltpu.with_memory_space_constraint(array, pltpu.HBM)


def fill_table(line_ref, table_ref, at):
    piece = line_ref[:, at : at + CHUNK + LANES]
    for tile in range(LANES // 16):
        moved = pltpu.roll(piece, 16 * tile, 1)[:, LANES:] if tile else piece[:, LANES:]
        for block in range(CHUNK // LANES):
            to_row = (block % 2) * LANES + 16 * tile
            to_col = (at // LANES + block) // 2 * LANES
            table_ref[to_row : to_row + 16, to_col : to_col + LANES] = moved[:, block * LANES : (block + 1) * LANES]


def pattern(values):
    row = lax.broadcasted_iota(jnp.int32, (8, LANES), 0) % len(values)
    tile = jnp.full((8, LANES), values[-1], f32)
    for index in range(len(values) - 1):
        tile = jnp.where(row == index, values[index], tile)
    return tile


def prepare_kernel(rank_ref, filter_ref, taps_ref, skip_ref, line_ref, tiles_ref, wide_ref):
    own = (rank_ref[0] * 4 // GROUP) % 8
    first = rank_ref[0] * 4
    wide_ref[:, : 2 * LANES] = jnp.zeros((8, 2 * LANES), f32)
    line_ref[:, :LANES] = jnp.zeros((16, LANES), bf16)
    for at in range(0, filter_ref.shape[1], CHUNK):
        piece = filter_ref[:, at : at + CHUNK].astype(f32)
        sub = lax.broadcasted_iota(jnp.int32, piece.shape, 0)
        chosen = jnp.sum(jnp.where(sub == own, piece, 0.0), axis=0, keepdims=True)
        wide_ref[:, 2 * LANES + at : 2 * LANES + at + CHUNK] = jnp.broadcast_to(chosen, piece.shape)
    for at in range(0, filter_ref.shape[1], CHUNK):
        piece = wide_ref[:, LANES + at : 2 * LANES + at + CHUNK]
        both = [pltpu.roll(piece, begin, 1, stride=1, stride_axis=0)[:, LANES:] for begin in (0, 8)]
        line_ref[:, LANES + at : LANES + at + CHUNK] = jnp.concatenate(both, axis=0).astype(bf16)
    for offset in range(3):
        tiles_ref[offset] = pattern([taps_ref[offset, feature, first + c] for feature in (1, 2) for c in range(4)])
    tiles_ref[3] = pattern([skip_ref[first + c] for c in range(4)])


def prepare(rank, filters, short_taps, skip_gain):
    seq_len = filters.shape[1]
    in_smem = pl.BlockSpec(memory_space=pltpu.SMEM)
    return pl.pallas_call(
        prepare_kernel,
        out_shape=[
            jax.ShapeDtypeStruct((16, LANES + seq_len), bf16),
            jax.ShapeDtypeStruct((4, 8, LANES), f32),
        ],
        grid_spec=pltpu.PrefetchScalarGridSpec(
            num_scalar_prefetch=1,
            grid=(1,),
            in_specs=[pl.BlockSpec((8, seq_len), lambda i, r: (r[0] * 4 // GROUP // 8, 0)), in_smem, in_smem],
            out_specs=[
                pl.BlockSpec((16, LANES + seq_len), lambda i, r: (0, 0)),
                pl.BlockSpec((4, 8, LANES), lambda i, r: (0, 0, 0)),
            ],
            scratch_shapes=[pltpu.VMEM((8, 2 * LANES + seq_len), f32)],
        ),
        compiler_params=params(16),
        cost_estimate=pl.CostEstimate(flops=1 << 22, bytes_accessed=1 << 20, transcendentals=0),
        name="prepare",
    )(rank, filters, short_taps, skip_gain)


def pack_kernel(features_ref, out_ref, rows_ref, packed_ref, in_sems, out_sems):
    rows = features_ref.shape[1] // PACK_STEPS
    fetches, stores = [], []
    for step in range(PACK_STEPS):
        here = slice(step * rows, (step + 1) * rows)
        fetches.append(pltpu.make_async_copy(features_ref.at[1:, here], rows_ref.at[:, here], in_sems.at[step]))
        fetches[-1].start()
    for step in range(PACK_STEPS):
        fetches[step].wait()
        k, v = (
            rows_ref[index, step * rows : (step + 1) * rows].astype(f32).reshape(rows // 8, 8, LANES) for index in range(2)
        )
        upper = lax.broadcasted_iota(jnp.int32, k.shape, 1) < 4
        even = jnp.where(upper, k, pltpu.roll(v, 4, 1))
        odd = jnp.where(upper, pltpu.roll(k, 4, 1), v)
        after = (step + PACK_STEPS // 2) % PACK_STEPS
        there = slice(after * rows // 4, (after + 1) * rows // 4)
        packed_ref[there] = jnp.stack([even, odd], axis=1).reshape(rows // 4, 8, LANES).astype(bf16)
        stores.append(pltpu.make_async_copy(packed_ref.at[there], out_ref.at[there], out_sems.at[step]))
        stores[-1].start()
    for store in stores:
        store.wait()


def pack(features):
    rows = features.shape[1]
    in_place = pl.BlockSpec(memory_space=pltpu.HBM)
    return pl.pallas_call(
        pack_kernel,
        out_shape=jax.ShapeDtypeStruct((rows // 4, 8, LANES), bf16),
        in_specs=[in_place],
        out_specs=in_place,
        scratch_shapes=[
            pltpu.VMEM((2, rows, LANES), bf16),
            pltpu.VMEM((rows // 4, 8, LANES), bf16),
            pltpu.SemaphoreType.DMA((PACK_STEPS,)),
            pltpu.SemaphoreType.DMA((PACK_STEPS,)),
        ],
        compiler_params=params(16),
        cost_estimate=pl.CostEstimate(flops=1 << 18, bytes_accessed=1 << 19, transcendentals=0),
        name="pack",
    )(features)


def conv_kernel(value_ref, line_ref, tiles_ref, out_ref, pair_ref, sum_ref, table_ref):
    blocks = value_ref.shape[0]
    rows = blocks * 4
    value = jnp.concatenate([value_ref[blocks // 2 :], value_ref[: blocks // 2]], axis=0).astype(f32)
    lane = lax.broadcasted_iota(jnp.int32, value.shape, 2)
    sub = lax.broadcasted_iota(jnp.int32, (blocks // 2, 8, LANES), 1)

    def delayed(array):
        return jnp.concatenate([jnp.zeros((1, 8, LANES), f32), array[:-1]], axis=0)

    conv = tiles_ref[0][None] * value
    for offset in (1, 2):
        turned = pltpu.roll(value, offset, 2)
        conv = conv + tiles_ref[offset][None] * jnp.where(lane < offset, delayed(turned), turned)
    kv = (conv * pltpu.roll(conv, 4, 1)).astype(bf16).astype(f32)
    kv = kv.reshape(blocks // 2, 2, 8, LANES)
    even, odd = kv[:, 0], kv[:, 1]
    pair_ref[:LEAD, :] = jnp.zeros((LEAD, 2 * LANES), bf16)
    pair_ref[LEAD:, :LANES] = jnp.where(sub < 4, even, odd).reshape(rows, LANES).astype(bf16)
    pair_ref[LEAD:, LANES:] = jnp.where(sub < 4, delayed(odd), even).reshape(rows, LANES).astype(bf16)

    direct = tiles_ref[3][None]
    sum_ref[...] = (pair_ref[LEAD:, :LANES].astype(f32).reshape(rows // 8, 8, LANES) * direct).reshape(rows, LANES)
    for index in range(rows // 64):
        begin, base = 64 * index, CHUNK * index
        for at in (2 * base, 2 * base + CHUNK):
            fill_table(line_ref, table_ref, at)
        left = [pair_ref[LEAD - 16 * s : LEAD - 16 * s + rows - begin, :] for s in range(4)]
        right = [table_ref[:, base + 256 * s : base + 256 * (s + 1)] for s in range(4)]
        moved = jnp.dot(
            jnp.concatenate(left, axis=1), jnp.concatenate(right, axis=0), preferred_element_type=f32
        )
        sum_ref[begin:, :] += moved[:, :LANES]
        sum_ref[begin + 8 :, :] += moved[: rows - begin - 8, LANES:]
    out_ref[: rows // 2, :] = sum_ref[rows // 2 :, :].astype(bf16)
    out_ref[rows // 2 :, :] = sum_ref[: rows // 2, :].astype(bf16)


def long_conv(value, line, tiles):
    rows = value.shape[0] * 4
    seq_len = line.shape[1] - LANES
    in_vmem = pl.BlockSpec(memory_space=pltpu.VMEM)
    return pl.pallas_call(
        conv_kernel,
        out_shape=jax.ShapeDtypeStruct((rows, LANES), bf16),
        in_specs=[in_vmem] * 3,
        out_specs=in_vmem,
        scratch_shapes=[
            pltpu.VMEM((LEAD + rows, 2 * LANES), bf16),
            pltpu.VMEM((rows, LANES), f32),
            pltpu.VMEM((2 * LANES, seq_len // 2), bf16),
        ],
        compiler_params=params(16),
        cost_estimate=pl.CostEstimate(flops=1 << 31, bytes_accessed=1 << 20, transcendentals=0),
        name="long_conv",
    )(value, line, tiles)


def turn_kernel(weight_ref, out_ref):
    out_ref[...] = jnp.transpose(weight_ref[...])


def turn(weight):
    width, total = weight.shape
    return pl.pallas_call(
        turn_kernel,
        out_shape=jax.ShapeDtypeStruct((total, width), bf16),
        grid=(total // width,),
        in_specs=[pl.BlockSpec((width, width), lambda i: (0, i))],
        out_specs=pl.BlockSpec((width, width), lambda i: (i, 0)),
        compiler_params=params(16),
        cost_estimate=pl.CostEstimate(flops=1 << 20, bytes_accessed=1 << 22, transcendentals=0),
        name="turn",
    )(weight)


def edge_kernel(rows_ref, out_ref):
    out_ref[...] = jnp.transpose(rows_ref[0])[LANES - 16 :, :]


def edge(features):
    channels, tokens = features.shape[1:]
    return pl.pallas_call(
        edge_kernel,
        out_shape=jax.ShapeDtypeStruct((16, channels), bf16),
        grid=(1,),
        in_specs=[pl.BlockSpec((1, channels, tokens), lambda i: (0, 0, 0))],
        out_specs=pl.BlockSpec((16, channels), lambda i: (0, 0)),
        compiler_params=params(16),
        cost_estimate=pl.CostEstimate(flops=1 << 16, bytes_accessed=1 << 17, transcendentals=0),
        name="edge",
    )(features)


def query_kernel(rows_ref, halo_ref, taps_ref, out_ref):
    value = rows_ref[0].astype(f32)
    lane = lax.broadcasted_iota(jnp.int32, value.shape, 1)
    halo = jnp.transpose(halo_ref[...].astype(f32))
    taps = taps_ref[:, 0, :]
    taps = jnp.transpose(jnp.concatenate([taps, jnp.zeros((5, taps.shape[1]), f32)], axis=0))
    once = jnp.where(lane == 0, halo[:, 15:16], pltpu.roll(value, 1, 1))
    twice = jnp.where(lane == 0, halo[:, 14:15], jnp.where(lane == 1, halo[:, 15:16], pltpu.roll(value, 2, 1)))
    out_ref[...] = taps[:, 0:1] * value + taps[:, 1:2] * once + taps[:, 2:3] * twice


def query_conv(features, halo, short_taps):
    channels, tokens = features.shape[1:]
    return pl.pallas_call(
        query_kernel,
        out_shape=jax.ShapeDtypeStruct((channels, tokens), f32),
        grid=(1,),
        in_specs=[
            pl.BlockSpec((1, channels, tokens), lambda i: (0, 0, 0)),
            pl.BlockSpec(halo.shape, lambda i: (0, 0)),
            pl.BlockSpec(short_taps.shape, lambda i: (0, 0, 0)),
        ],
        out_specs=pl.BlockSpec((channels, tokens), lambda i: (0, 0)),
        compiler_params=params(16),
        cost_estimate=pl.CostEstimate(flops=1 << 20, bytes_accessed=1 << 19, transcendentals=0),
        name="query_conv",
    )(features, halo, short_taps)


def gated_of(q_ref, mix_ref):
    half = mix_ref.shape[0] // 2
    mix = jnp.concatenate([mix_ref[half:, :], mix_ref[:half, :]], axis=0)
    return (q_ref[...] * mix.astype(f32)).astype(bf16)


def own_part(member, q_ref, mix_ref, weight_ref):
    width = mix_ref.shape[0]
    at = pl.multiple_of(member * width, width)
    return jnp.dot(weight_ref[pl.ds(at, width), :], gated_of(q_ref, mix_ref), preferred_element_type=f32)


def give_kernel(member_ref, q_ref, mix_ref, weight_ref, out_ref):
    out_ref[...] = own_part(member_ref[0], q_ref, mix_ref, weight_ref).astype(bf16)


def keep_kernel(member_ref, q_ref, mix_ref, weight_ref, given_ref, out_ref):
    own = own_part(member_ref[0], q_ref, mix_ref, weight_ref)
    out_ref[...] = (own + given_ref[...].astype(f32)).astype(out_ref.dtype)


def project(kernel, member, operands, rows, kind):
    in_vmem = pl.BlockSpec(memory_space=pltpu.VMEM)
    return pl.pallas_call(
        kernel,
        out_shape=jax.ShapeDtypeStruct((rows, operands[1].shape[1]), kind),
        in_specs=[pl.BlockSpec(memory_space=pltpu.SMEM)] + [in_vmem] * len(operands),
        out_specs=in_vmem,
        compiler_params=params(16),
        cost_estimate=pl.CostEstimate(flops=1 << 27, bytes_accessed=1 << 21, transcendentals=0),
    )(member, *operands)


def local(features, short_taps, filters, skip_gain, out_weight):
    chan_tp, tok_local = features.shape[1:]
    ctx_count = lax.axis_size("ctx")
    chan_dev = chan_tp // ctx_count
    rank = jnp.full((1,), lax.axis_index("ctx"), jnp.int32)
    member = jnp.full((1,), lax.axis_index("tp"), jnp.int32)

    sent = pack(in_hbm(features))
    order = [(i + ctx_count // 2) % ctx_count for i in range(ctx_count)]
    got = lax.all_to_all(sent, "ctx", 0, 0, axis_index_groups=[order], tiled=True)
    line, tiles = prepare(rank, *map(in_hbm, (filters, short_taps, skip_gain)))
    last = edge(in_hbm(features))
    halo = lax.ppermute(last, "ctx", [(i, i + 1) for i in range(ctx_count - 1)])
    mix = long_conv(got, line, tiles).reshape(ctx_count, chan_dev, tok_local)
    mix = lax.all_to_all(mix, "ctx", 0, 0, axis_index_groups=[order], tiled=True).reshape(chan_tp, tok_local)
    q = query_conv(features, halo, short_taps)
    weight = turn(in_hbm(out_weight))
    operands = (q, mix, weight)
    rows = chan_tp
    given = project(give_kernel, lax.bitwise_xor(member, 3), operands, rows, bf16)
    given = lax.ppermute(given, "tp", CORE_PAIRS)
    away = project(keep_kernel, lax.bitwise_xor(member, 2), (*operands, given), rows, bf16)
    arrived = lax.ppermute(away, "tp", CHIP_PAIRS)
    given_home = project(give_kernel, lax.bitwise_xor(member, 1), operands, rows, bf16)
    given_home = lax.ppermute(given_home, "tp", CORE_PAIRS)
    home = project(keep_kernel, member, (*operands, given_home), rows, f32)
    return (home + arrived.astype(f32)).astype(bf16)


def solution(mesh):
    placed = (P(None, "tp", "ctx"), P(None, None, "tp"), P("tp", None), P("tp"), P("tp", None))
    return jax.shard_map(
        local, mesh=mesh, in_specs=placed, out_specs=P("tp", "ctx"), check_vma=False
    )
```

```python
import jax
import jax.numpy as jnp
from jax import lax
from jax.experimental import pallas as pl
from jax.experimental.pallas import tpu as pltpu
from jax.sharding import PartitionSpec as P


GROUP = 16
LANES = 128
CHUNK = 1024
LEAD = 48
PACK_STEPS = 4
CORE_PAIRS = [(0, 1), (1, 0), (2, 3), (3, 2)]
CHIP_PAIRS = [(0, 2), (2, 0), (1, 3), (3, 1)]

f32 = jnp.float32
bf16 = jnp.bfloat16


def params(mib):
    return pltpu.CompilerParams(vmem_limit_bytes=mib << 20)


def swapped(array, pieces=32, flip=19):
    size = array.shape[0] // pieces
    return jnp.concatenate([array[(i ^ flip) * size : ((i ^ flip) + 1) * size] for i in range(pieces)], axis=0)


def in_hbm(array):
    return pltpu.with_memory_space_constraint(array, pltpu.HBM)


def fill_table(line_ref, table_ref, at):
    piece = line_ref[:, at : at + CHUNK + LANES]
    for tile in range(LANES // 16):
        moved = pltpu.roll(piece, 16 * tile, 1)[:, LANES:] if tile else piece[:, LANES:]
        for block in range(CHUNK // LANES):
            to_row = (block % 2) * LANES + 16 * tile
            to_col = (at // LANES + block) // 2 * LANES
            table_ref[to_row : to_row + 16, to_col : to_col + LANES] = moved[:, block * LANES : (block + 1) * LANES]


def pattern(values):
    row = lax.broadcasted_iota(jnp.int32, (8, LANES), 0) % len(values)
    tile = jnp.full((8, LANES), values[-1], f32)
    for index in range(len(values) - 1):
        tile = jnp.where(row == index, values[index], tile)
    return tile


def prepare_kernel(rank_ref, filter_ref, taps_ref, skip_ref, line_ref, tiles_ref, wide_ref):
    own = (rank_ref[0] * 4 // GROUP) % 8
    first = rank_ref[0] * 4
    wide_ref[:, : 2 * LANES] = jnp.zeros((8, 2 * LANES), f32)
    line_ref[:, :LANES] = jnp.zeros((16, LANES), bf16)
    for at in range(0, filter_ref.shape[1], CHUNK):
        piece = filter_ref[:, at : at + CHUNK].astype(f32)
        sub = lax.broadcasted_iota(jnp.int32, piece.shape, 0)
        chosen = jnp.sum(jnp.where(sub == own, piece, 0.0), axis=0, keepdims=True)
        wide_ref[:, 2 * LANES + at : 2 * LANES + at + CHUNK] = jnp.broadcast_to(chosen, piece.shape)
    for at in range(0, filter_ref.shape[1], CHUNK):
        piece = wide_ref[:, LANES + at : 2 * LANES + at + CHUNK]
        both = [pltpu.roll(piece, begin, 1, stride=1, stride_axis=0)[:, LANES:] for begin in (0, 8)]
        line_ref[:, LANES + at : LANES + at + CHUNK] = jnp.concatenate(both, axis=0).astype(bf16)
    for offset in range(3):
        tiles_ref[offset] = pattern([taps_ref[offset, feature, first + c] for feature in (1, 2) for c in range(4)])
    tiles_ref[3] = pattern([skip_ref[first + c] for c in range(4)])


def prepare(rank, filters, short_taps, skip_gain):
    seq_len = filters.shape[1]
    in_smem = pl.BlockSpec(memory_space=pltpu.SMEM)
    return pl.pallas_call(
        prepare_kernel,
        out_shape=[
            jax.ShapeDtypeStruct((16, LANES + seq_len), bf16),
            jax.ShapeDtypeStruct((4, 8, LANES), f32),
        ],
        grid_spec=pltpu.PrefetchScalarGridSpec(
            num_scalar_prefetch=1,
            grid=(1,),
            in_specs=[pl.BlockSpec((8, seq_len), lambda i, r: (r[0] * 4 // GROUP // 8, 0)), in_smem, in_smem],
            out_specs=[
                pl.BlockSpec((16, LANES + seq_len), lambda i, r: (0, 0)),
                pl.BlockSpec((4, 8, LANES), lambda i, r: (0, 0, 0)),
            ],
            scratch_shapes=[pltpu.VMEM((8, 2 * LANES + seq_len), f32)],
        ),
        compiler_params=params(16),
        cost_estimate=pl.CostEstimate(flops=1 << 22, bytes_accessed=1 << 20, transcendentals=0),
        name="prepare",
    )(rank, filters, short_taps, skip_gain)


def pack_kernel(features_ref, out_ref, rows_ref, packed_ref, in_sems, out_sems):
    rows = features_ref.shape[1] // PACK_STEPS
    fetches, stores = [], []
    for step in range(PACK_STEPS):
        here = slice(step * rows, (step + 1) * rows)
        fetches.append(pltpu.make_async_copy(features_ref.at[1:, here], rows_ref.at[:, here], in_sems.at[step]))
        fetches[-1].start()
    for step in range(PACK_STEPS):
        fetches[step].wait()
        k, v = (
            rows_ref[index, step * rows : (step + 1) * rows].astype(f32).reshape(rows // 8, 8, LANES) for index in range(2)
        )
        upper = lax.broadcasted_iota(jnp.int32, k.shape, 1) < 4
        even = jnp.where(upper, k, pltpu.roll(v, 4, 1))
        odd = jnp.where(upper, pltpu.roll(k, 4, 1), v)
        after = (step + PACK_STEPS // 2) % PACK_STEPS
        there = slice(after * rows // 4, (after + 1) * rows // 4)
        packed_ref[there] = swapped(jnp.stack([even, odd], axis=1).reshape(rows // 4, 8, LANES), 8, 3).astype(bf16)
        stores.append(pltpu.make_async_copy(packed_ref.at[there], out_ref.at[there], out_sems.at[step]))
        stores[-1].start()
    for store in stores:
        store.wait()


def pack(features):
    rows = features.shape[1]
    in_place = pl.BlockSpec(memory_space=pltpu.HBM)
    return pl.pallas_call(
        pack_kernel,
        out_shape=jax.ShapeDtypeStruct((rows // 4, 8, LANES), bf16),
        in_specs=[in_place],
        out_specs=in_place,
        scratch_shapes=[
            pltpu.VMEM((2, rows, LANES), bf16),
            pltpu.VMEM((rows // 4, 8, LANES), bf16),
            pltpu.SemaphoreType.DMA((PACK_STEPS,)),
            pltpu.SemaphoreType.DMA((PACK_STEPS,)),
        ],
        compiler_params=params(16),
        cost_estimate=pl.CostEstimate(flops=1 << 18, bytes_accessed=1 << 19, transcendentals=0),
        name="pack",
    )(features)


def conv_kernel(value_ref, line_ref, tiles_ref, out_ref, pair_ref, sum_ref, table_ref):
    blocks = value_ref.shape[0]
    rows = blocks * 4
    value = swapped(value_ref[...].astype(f32))
    lane = lax.broadcasted_iota(jnp.int32, value.shape, 2)
    sub = lax.broadcasted_iota(jnp.int32, (blocks // 2, 8, LANES), 1)

    def delayed(array):
        return jnp.concatenate([jnp.zeros((1, 8, LANES), f32), array[:-1]], axis=0)

    conv = tiles_ref[0][None] * value
    for offset in (1, 2):
        turned = pltpu.roll(value, offset, 2)
        conv = conv + tiles_ref[offset][None] * jnp.where(lane < offset, delayed(turned), turned)
    kv = (conv * pltpu.roll(conv, 4, 1)).astype(bf16).astype(f32)
    kv = kv.reshape(blocks // 2, 2, 8, LANES)
    even, odd = kv[:, 0], kv[:, 1]
    pair_ref[:LEAD, :] = jnp.zeros((LEAD, 2 * LANES), bf16)
    pair_ref[LEAD:, :LANES] = jnp.where(sub < 4, even, odd).reshape(rows, LANES).astype(bf16)
    pair_ref[LEAD:, LANES:] = jnp.where(sub < 4, delayed(odd), even).reshape(rows, LANES).astype(bf16)

    direct = tiles_ref[3][None]
    sum_ref[...] = (pair_ref[LEAD:, :LANES].astype(f32).reshape(rows // 8, 8, LANES) * direct).reshape(rows, LANES)
    for index in range(rows // 64):
        begin, base = 64 * index, CHUNK * index
        for at in (2 * base, 2 * base + CHUNK):
            fill_table(line_ref, table_ref, at)
        left = [pair_ref[LEAD - 16 * s : LEAD - 16 * s + rows - begin, :] for s in range(4)]
        right = [table_ref[:, base + 256 * s : base + 256 * (s + 1)] for s in range(4)]
        moved = jnp.dot(
            jnp.concatenate(left, axis=1), jnp.concatenate(right, axis=0), preferred_element_type=f32
        )
        sum_ref[begin:, :] += moved[:, :LANES]
        sum_ref[begin + 8 :, :] += moved[: rows - begin - 8, LANES:]
    out_ref[...] = swapped(sum_ref[...]).astype(bf16)


def long_conv(value, line, tiles):
    rows = value.shape[0] * 4
    seq_len = line.shape[1] - LANES
    in_vmem = pl.BlockSpec(memory_space=pltpu.VMEM)
    return pl.pallas_call(
        conv_kernel,
        out_shape=jax.ShapeDtypeStruct((rows, LANES), bf16),
        in_specs=[in_vmem] * 3,
        out_specs=in_vmem,
        scratch_shapes=[
            pltpu.VMEM((LEAD + rows, 2 * LANES), bf16),
            pltpu.VMEM((rows, LANES), f32),
            pltpu.VMEM((2 * LANES, seq_len // 2), bf16),
        ],
        compiler_params=params(16),
        cost_estimate=pl.CostEstimate(flops=1 << 31, bytes_accessed=1 << 20, transcendentals=0),
        name="long_conv",
    )(value, line, tiles)


def turn_kernel(weight_ref, out_ref):
    out_ref[...] = jnp.transpose(weight_ref[...])


def turn(weight):
    width, total = weight.shape
    return pl.pallas_call(
        turn_kernel,
        out_shape=jax.ShapeDtypeStruct((total, width), bf16),
        grid=(total // width,),
        in_specs=[pl.BlockSpec((width, width), lambda i: (0, i))],
        out_specs=pl.BlockSpec((width, width), lambda i: (i, 0)),
        compiler_params=params(16),
        cost_estimate=pl.CostEstimate(flops=1 << 20, bytes_accessed=1 << 22, transcendentals=0),
        name="turn",
    )(weight)


def edge_kernel(rows_ref, out_ref):
    out_ref[...] = jnp.transpose(rows_ref[0])[LANES - 16 :, :]


def edge(features):
    channels, tokens = features.shape[1:]
    return pl.pallas_call(
        edge_kernel,
        out_shape=jax.ShapeDtypeStruct((16, channels), bf16),
        grid=(1,),
        in_specs=[pl.BlockSpec((1, channels, tokens), lambda i: (0, 0, 0))],
        out_specs=pl.BlockSpec((16, channels), lambda i: (0, 0)),
        compiler_params=params(16),
        cost_estimate=pl.CostEstimate(flops=1 << 16, bytes_accessed=1 << 17, transcendentals=0),
        name="edge",
    )(features)


def query_kernel(rows_ref, halo_ref, taps_ref, out_ref):
    value = rows_ref[0].astype(f32)
    lane = lax.broadcasted_iota(jnp.int32, value.shape, 1)
    halo = jnp.transpose(halo_ref[...].astype(f32))
    taps = taps_ref[:, 0, :]
    taps = jnp.transpose(jnp.concatenate([taps, jnp.zeros((5, taps.shape[1]), f32)], axis=0))
    once = jnp.where(lane == 0, halo[:, 15:16], pltpu.roll(value, 1, 1))
    twice = jnp.where(lane == 0, halo[:, 14:15], jnp.where(lane == 1, halo[:, 15:16], pltpu.roll(value, 2, 1)))
    out_ref[...] = taps[:, 0:1] * value + taps[:, 1:2] * once + taps[:, 2:3] * twice


def query_conv(features, halo, short_taps):
    channels, tokens = features.shape[1:]
    return pl.pallas_call(
        query_kernel,
        out_shape=jax.ShapeDtypeStruct((channels, tokens), f32),
        grid=(1,),
        in_specs=[
            pl.BlockSpec((1, channels, tokens), lambda i: (0, 0, 0)),
            pl.BlockSpec(halo.shape, lambda i: (0, 0)),
            pl.BlockSpec(short_taps.shape, lambda i: (0, 0, 0)),
        ],
        out_specs=pl.BlockSpec((channels, tokens), lambda i: (0, 0)),
        compiler_params=params(16),
        cost_estimate=pl.CostEstimate(flops=1 << 20, bytes_accessed=1 << 19, transcendentals=0),
        name="query_conv",
    )(features, halo, short_taps)


def gated_of(q_ref, mix_ref):
    return (q_ref[...] * swapped(mix_ref[...].astype(f32))).astype(bf16)


def own_part(member, q_ref, mix_ref, weight_ref):
    width = mix_ref.shape[0]
    at = pl.multiple_of(member * width, width)
    return jnp.dot(weight_ref[pl.ds(at, width), :], gated_of(q_ref, mix_ref), preferred_element_type=f32)


def give_kernel(member_ref, q_ref, mix_ref, weight_ref, out_ref):
    out_ref[...] = own_part(member_ref[0], q_ref, mix_ref, weight_ref).astype(bf16)


def keep_kernel(member_ref, q_ref, mix_ref, weight_ref, given_ref, out_ref):
    own = own_part(member_ref[0], q_ref, mix_ref, weight_ref)
    out_ref[...] = (own + given_ref[...].astype(f32)).astype(out_ref.dtype)


def project(kernel, member, operands, rows, kind):
    in_vmem = pl.BlockSpec(memory_space=pltpu.VMEM)
    return pl.pallas_call(
        kernel,
        out_shape=jax.ShapeDtypeStruct((rows, operands[1].shape[1]), kind),
        in_specs=[pl.BlockSpec(memory_space=pltpu.SMEM)] + [in_vmem] * len(operands),
        out_specs=in_vmem,
        compiler_params=params(16),
        cost_estimate=pl.CostEstimate(flops=1 << 27, bytes_accessed=1 << 21, transcendentals=0),
    )(member, *operands)


def local(features, short_taps, filters, skip_gain, out_weight):
    chan_tp, tok_local = features.shape[1:]
    ctx_count = lax.axis_size("ctx")
    chan_dev = chan_tp // ctx_count
    rank = jnp.full((1,), lax.axis_index("ctx"), jnp.int32)
    member = jnp.full((1,), lax.axis_index("tp"), jnp.int32)

    sent = pack(in_hbm(features))
    order = [i ^ 76 for i in range(ctx_count)]
    got = lax.all_to_all(sent, "ctx", 0, 0, axis_index_groups=[order], tiled=True)
    line, tiles = prepare(rank, *map(in_hbm, (filters, short_taps, skip_gain)))
    last = edge(in_hbm(features))
    halo = lax.ppermute(last, "ctx", [(i, i + 1) for i in range(ctx_count - 1)])
    mix = long_conv(got, line, tiles).reshape(ctx_count, chan_dev, tok_local)
    mix = lax.all_to_all(mix, "ctx", 0, 0, axis_index_groups=[order], tiled=True).reshape(chan_tp, tok_local)
    q = query_conv(features, halo, short_taps)
    weight = turn(in_hbm(out_weight))
    operands = (q, mix, weight)
    rows = chan_tp
    given = project(give_kernel, lax.bitwise_xor(member, 3), operands, rows, bf16)
    given = lax.ppermute(given, "tp", CORE_PAIRS)
    away = project(keep_kernel, lax.bitwise_xor(member, 2), (*operands, given), rows, bf16)
    arrived = lax.ppermute(away, "tp", CHIP_PAIRS)
    given_home = project(give_kernel, lax.bitwise_xor(member, 1), operands, rows, bf16)
    given_home = lax.ppermute(given_home, "tp", CORE_PAIRS)
    home = project(keep_kernel, member, (*operands, given_home), rows, f32)
    return (home + arrived.astype(f32)).astype(bf16)


def solution(mesh):
    placed = (P(None, "tp", "ctx"), P(None, None, "tp"), P("tp", None), P("tp"), P("tp", None))
    return jax.shard_map(
        local, mesh=mesh, in_specs=placed, out_specs=P("tp", "ctx"), check_vma=False
    )
```
